512 devices in a mesh: space: 32 (over y, z_hi), tensor: 16 (over x, z_lo, core).
Axes of the slice: x: 4, y: 8, z: 8 (z_hi: 4, z_lo: 2; z = z_hi * 2 + z_lo), core: 2. Of those that a mesh axis runs over, the one named last changes fastest.
Arguments:
- features: bfloat16 [128, 128, 1024], P('space', None, 'tensor'), may hold values from -6 to 6
- depth_kernel: bfloat16 [2, 7, 7, 1024], P(None, None, None, 'tensor'), may hold values from -5 to 5
- norm_gain: float32 [2, 1024], replicated, may hold values from 0.5 to 1.5
- norm_bias: float32 [2, 1024], replicated, may hold values from -3 to 3
- w_expand: bfloat16 [2, 1024, 4096], P(None, None, 'tensor'), may hold values from -0.1875 to 0.1875
- b_expand: float32 [2, 4096], P(None, 'tensor'), may hold values from -3 to 3
- w_reduce: bfloat16 [2, 4096, 1024], P(None, 'tensor'), may hold values from -0.125 to 0.125
- b_reduce: float32 [2, 1024], P(None, 'tensor'), may hold values from -3 to 3
- layer_scale: float32 [2, 1024], P(None, 'tensor'), may hold values from 0.5 to 1.5
Outputs:
- output: bfloat16 [128, 128, 1024], P('space', None, 'tensor')
The draws below stay inside these ranges and needn't reach their ends.
All inputs are finite; a program needn't handle non-finite values.
Results may differ from the reference program's by a relative error of at most 0.023.
Values may be sent and summed in bfloat16 or wider, within the bound.
No kernel may reach another device: no remote copies, remote signals or barrier semaphores. Data moves between devices by JAX's collectives and lax.ppermute only.
A program may use at most 64 MiB of HBM per device.

```python
import jax
import jax.numpy as jnp
from jax import lax

D = 1024
FF = 4096
TAPS = 7
BLOCKS = 2
COLS = 128
ROWS = 128
N_TENSOR = 16


def draw_depth_kernel(key, part):
    key_base, key_jitter = jax.random.split(jax.random.fold_in(key, 7))
    base = jnp.clip(jax.random.normal(key_base, (BLOCKS, TAPS, TAPS, D), jnp.float32), -4.0, 4.0) / 7.0
    jitter = jax.random.uniform(key_jitter, (BLOCKS, 1, 1, D), jnp.float32, 0.8, 1.25)
    ladder = jnp.arange(D, dtype=jnp.float32) / D
    scale = 0.3 * jnp.power(10.0, ladder) * jitter
    return (base * scale).astype(jnp.bfloat16)


def strengthened(entries, own_key, source, target, parts, factor):
    def block_of(dim):
        return (jnp.arange(entries.shape[dim]) // (entries.shape[dim] // parts)).reshape((-1,) + (1,) * (entries.ndim - 1 - dim))

    near = jax.random.permutation(own_key, parts)[block_of(target)]
    second = (block_of(target) + parts // 2) % parts
    return jnp.where((block_of(source) == near) | (block_of(source) == second), factor * entries, entries)


def shard_levels(key, extent, shards, least, largest):
    level, own = 1.0, jax.random.fold_in(key, 6)
    for axis_at, shards_of in shards:
        draws = jnp.exp(jax.random.uniform(jax.random.fold_in(own, axis_at), (shards_of,), jnp.float32, least / len(shards), largest / len(shards)))
        level = level * jnp.repeat(draws, extent[axis_at] // shards_of).reshape([-1 if axis == axis_at else 1 for axis in range(len(extent))])
    return level


def scatter_about(own_key, dims, deviation, reach, cuts=(), kind=jnp.bfloat16):
    factor_of = shard_levels(own_key, dims, cuts, -0.22, 0.18) if cuts else 1.0
    drawn = jax.random.normal(own_key, dims, jnp.float32) * deviation * factor_of
    return jnp.minimum(jnp.maximum(drawn, -reach), reach).astype(kind)


def noise_with(rng, shape, spread, limit, cuts, heavy, held_as=jnp.bfloat16):
    values = spread * jax.random.normal(rng, shape, jnp.float32)
    if cuts:
        values = values * shard_levels(rng, shape, cuts, -0.22, 0.18)
    return jnp.clip(strengthened(values, jax.random.fold_in(rng, 3), *heavy), -limit, limit).astype(held_as)


def setup_inputs(seed: int = 0) -> dict:
    splits = jax.random.split(jax.random.key(seed), 10)
    return {
        "features": scatter_about(splits[0], (ROWS, COLS, D), 1.0, 6.0, ((0, 32), (2, 16))),
        "depth_kernel": draw_depth_kernel(jax.random.fold_in(splits[9], 71), 0),
        "norm_gain": jnp.clip(jax.random.uniform(splits[2], (BLOCKS, D), jnp.float32, 0.5, 1.5), 0.5, 1.5),
        "norm_bias": scatter_about(splits[3], (BLOCKS, D), 0.5, 3.0, (), jnp.float32),
        "w_expand": scatter_about(splits[4], (BLOCKS, D, FF), D ** -0.5, 0.1875, ((2, 16),)),
        "b_expand": scatter_about(splits[5], (BLOCKS, FF), 0.5, 3.0, ((1, 16),), jnp.float32),
        "w_reduce": noise_with(splits[6], (BLOCKS, FF, D), FF ** -0.5, 0.125, ((1, 16),), (1, 2, 16, 2.0)),
        "b_reduce": scatter_about(splits[7], (BLOCKS, D), 0.5, 3.0, ((1, 16),), jnp.float32),
        "layer_scale": jnp.clip(0.5 + 1.0 * jax.random.uniform(splits[8], (BLOCKS, D), jnp.float32) ** shard_levels(splits[8], (BLOCKS, D), ((1, 16),), -0.2, 0.2), 0.5, 1.5),
    }


def depthwise(stream, kernel):
    half = TAPS // 2
    height = stream.shape[0]
    width = stream.shape[1]
    padded = jnp.pad(stream.astype(jnp.float32), ((half, half), (half, half), (0, 0)))
    total = jnp.zeros(stream.shape, jnp.float32)
    for row_tap in range(TAPS):
        for col_tap in range(TAPS):
            total = total + padded[row_tap:row_tap + height, col_tap:col_tap + width] * kernel[row_tap, col_tap].astype(jnp.float32)
    return total

def reference(features, depth_kernel, norm_gain, norm_bias, w_expand, b_expand, w_reduce, b_reduce, layer_scale):
    stream = features
    group = FF // N_TENSOR
    for block_id in range(BLOCKS):
        filtered = depthwise(stream, depth_kernel[block_id])
        mean = lax.optimization_barrier(jnp.mean(filtered, axis=-1, keepdims=True))
        centered = filtered - mean
        var = lax.optimization_barrier(jnp.mean(centered * centered, axis=-1, keepdims=True))
        normed = (centered / jnp.sqrt(var + 1e-06) * norm_gain[block_id] + norm_bias[block_id]).astype(jnp.bfloat16)
        reduce_groups = w_reduce[block_id].astype(jnp.float32).reshape(N_TENSOR, group, D)
        expand = w_expand[block_id]
        bias_one = b_expand[block_id]

        def one_row(row_normed):
            preact = jnp.dot(row_normed, expand, preferred_element_type=jnp.float32) + bias_one
            hidden = jax.nn.gelu(preact, approximate=False).astype(jnp.bfloat16)
            grouped = hidden.astype(jnp.float32).reshape(row_normed.shape[0], N_TENSOR, group)
            partial_value = jnp.einsum('wtf,tfc->wtc', grouped, reduce_groups)
            partial_value = lax.optimization_barrier(partial_value.astype(jnp.bfloat16))
            return lax.optimization_barrier(jnp.sum(partial_value.astype(jnp.float32), axis=1))
        mixed = lax.map(one_row, normed)
        stream = (stream.astype(jnp.float32) + layer_scale[block_id] * (mixed + b_reduce[block_id])).astype(jnp.bfloat16)
    return stream
```

```python
import jax
import jax.numpy as jnp
from jax import lax
from jax.experimental import pallas as pl
from jax.experimental.pallas import tpu as pltpu
from jax.sharding import PartitionSpec as P

D = 1024
TAPS = 7
HALF = TAPS // 2
BLOCKS = 2
CORES = 2

VMEM = pl.BlockSpec(memory_space=pltpu.VMEM)


def call(body, outs, *args):
    single = not isinstance(outs, (list, tuple))
    return pl.pallas_call(
        body,
        out_shape=outs,
        in_specs=[VMEM] * len(args),
        out_specs=VMEM if single else [VMEM] * len(outs),
        compiler_params=pltpu.CompilerParams(vmem_limit_bytes=48 << 20),
    )(*args)


def conv_kernel(before_ref, rows_ref, after_ref, taps_ref, out_ref):
    height, share, width = rows_ref.shape
    copies = out_ref.shape[0]
    column = lax.broadcasted_iota(jnp.int32, (8, width), 1)
    for group in range(share // 8):
        chans = slice(8 * group, 8 * group + 8)
        rows = [before_ref[r, chans, :] for r in range(HALF)]
        rows += [rows_ref[r, chans, :] for r in range(height)]
        rows += [after_ref[r, chans, :] for r in range(HALF)]
        rows = [row.astype(jnp.float32) for row in rows]
        totals = [jnp.zeros((8, width), jnp.float32)] * height
        for j in range(TAPS):
            taps = [
                jnp.broadcast_to(taps_ref[chans, i * TAPS + j : i * TAPS + j + 1], (8, width))
                for i in range(TAPS)
            ]
            shift = j - HALF
            for r in range(height):
                acc = rows[r] * taps[0]
                for i in range(1, TAPS):
                    acc = acc + rows[r + i] * taps[i]
                if shift:
                    acc = pltpu.roll(acc, (-shift) % width, 1)
                    inside = (column + shift >= 0) & (column + shift < width)
                    acc = jnp.where(inside, acc, 0.0)
                totals[r] = totals[r] + acc
        for r in range(height):
            half, at = divmod(r, height // CORES)
            value = totals[r].astype(jnp.bfloat16)
            for copy in range(copies):
                out_ref[copy, half, chans, width * at : width * (at + 1)] = value


def mlp_kernel(block, x_ref, gain_ref, bias_ref, ea_ref, eb_ref, ba_ref, bb_ref, ra_ref, rb_ref, out_ref):
    x = x_ref[...].reshape(D, x_ref.shape[-1])
    x = jnp.transpose(x).astype(jnp.float32)
    mean = jnp.mean(x, axis=-1, keepdims=True)
    centered = x - mean
    var = jnp.mean(centered * centered, axis=-1, keepdims=True)
    gain = gain_ref[block : block + 1, :]
    bias = bias_ref[block : block + 1, :]
    normed = (centered * lax.rsqrt(var + 1e-06) * gain + bias).astype(jnp.bfloat16)
    total = None
    for e_ref, b_ref, r_ref in ((ea_ref, ba_ref, ra_ref), (eb_ref, bb_ref, rb_ref)):
        preact = jnp.dot(normed, e_ref[block], preferred_element_type=jnp.float32)
        preact = preact + b_ref[block : block + 1, :]
        hidden = 0.5 * preact * (1.0 + lax.erf(preact * (0.5**0.5)))
        partial = jnp.dot(hidden.astype(jnp.bfloat16), r_ref[block], preferred_element_type=jnp.float32)
        total = partial if total is None else total + partial
    out_ref[...] = jnp.transpose(total.astype(jnp.bfloat16)).reshape(out_ref.shape)


def mix_rows(block, parts_ref, stream_ref, cols_ref):
    height, share, width = stream_ref.shape
    scale = jnp.broadcast_to(cols_ref[:, 2 * block : 2 * block + 1], (share, width))
    shift = jnp.broadcast_to(cols_ref[:, 2 * block + 1 : 2 * block + 2], (share, width))
    rows = []
    for r in range(height):
        half, at = divmod(r, height // CORES)
        lanes = slice(width * at, width * (at + 1))
        mixed = parts_ref[0, half, :, lanes].astype(jnp.float32)
        for copy in range(1, parts_ref.shape[0]):
            mixed = mixed + parts_ref[copy, half, :, lanes].astype(jnp.float32)
        updated = stream_ref[r].astype(jnp.float32) + scale * (mixed + shift)
        rows.append(updated.astype(jnp.bfloat16))
    return rows


def mix_kernel(block, parts_ref, stream_ref, cols_ref, out_ref, first_ref, last_ref):
    rows = mix_rows(block, parts_ref, stream_ref, cols_ref)
    for r, row in enumerate(rows):
        out_ref[r] = row
        if r < HALF:
            first_ref[r] = row
        if r >= len(rows) - HALF:
            last_ref[r - (len(rows) - HALF)] = row


def last_kernel(block, parts_ref, stream_ref, cols_ref, out_ref):
    for r, row in enumerate(mix_rows(block, parts_ref, stream_ref, cols_ref)):
        out_ref[r] = row


def per_device(features, depth_kernel, norm_gain, norm_bias, w_expand, b_expand, w_reduce, b_reduce, layer_scale):
    height, width, share = features.shape
    bands, members = lax.axis_size("space"), lax.axis_size("tensor")
    copies = members // CORES
    half = height // CORES * width
    down = [(i, i + 1) for i in range(bands - 1)]
    up = [(j, i) for i, j in down]
    sibling = [(i, i ^ 1) for i in range(members)]

    stream = jnp.transpose(features, (0, 2, 1))
    first, last = stream[:HALF], stream[height - HALF :]
    before = lax.ppermute(last, "space", down)
    after = lax.ppermute(first, "space", up)
    other_expand = lax.ppermute(w_expand, "tensor", sibling)
    other_reduce = lax.ppermute(w_reduce, "tensor", sibling)
    other_bias = lax.ppermute(b_expand, "tensor", sibling)
    taps = jnp.transpose(depth_kernel.reshape(BLOCKS, TAPS * TAPS, share), (0, 2, 1)).astype(jnp.float32)
    cols = jnp.stack([layer_scale[0], b_reduce[0], layer_scale[1], b_reduce[1]], axis=-1)

    for block in range(BLOCKS):
        filtered = call(
            conv_kernel,
            jax.ShapeDtypeStruct((copies, CORES, share, half), jnp.bfloat16),
            before, stream, after, taps[block],
        )
        filtered = lax.all_to_all(filtered.reshape(members, share, half), "tensor", 0, 0, tiled=True)
        partial = call(
            lambda *refs: mlp_kernel(block, *refs),
            jax.ShapeDtypeStruct((members, share, half), jnp.bfloat16),
            filtered, norm_gain, norm_bias, w_expand, other_expand, b_expand, other_bias, w_reduce, other_reduce,
        )
        partial = lax.all_to_all(partial, "tensor", 0, 0, tiled=True).reshape(copies, CORES, share, half)
        whole = jax.ShapeDtypeStruct((height, share, width), jnp.bfloat16)
        if block == BLOCKS - 1:
            stream = call(lambda *refs: last_kernel(block, *refs), whole, partial, stream, cols)
        else:
            edge = jax.ShapeDtypeStruct((HALF, share, width), jnp.bfloat16)
            stream, first, last = call(
                lambda *refs: mix_kernel(block, *refs), (whole, edge, edge), partial, stream, cols
            )
            before = lax.ppermute(last, "space", down)
            after = lax.ppermute(first, "space", up)
    return jnp.transpose(stream, (0, 2, 1))


def solution(mesh):
    return jax.shard_map(
        per_device,
        mesh=mesh,
        in_specs=(
            P("space", None, "tensor"),
            P(None, None, None, "tensor"),
            P(),
            P(),
            P(None, None, "tensor"),
            P(None, "tensor"),
            P(None, "tensor", None),
            P(None, "tensor"),
            P(None, "tensor"),
        ),
        out_specs=P("space", None, "tensor"),
        check_vma=False,
    )
```

```python
import jax
import jax.numpy as jnp
from jax import lax
from jax.experimental import pallas as pl
from jax.experimental.pallas import tpu as pltpu
from jax.sharding import PartitionSpec as P

D = 1024
TAPS = 7
HALF = TAPS // 2
BLOCKS = 2
CORES = 2

VMEM = pl.BlockSpec(memory_space=pltpu.VMEM)


def call(body, outs, *args):
    single = not isinstance(outs, (list, tuple))
    return pl.pallas_call(
        body,
        out_shape=outs,
        in_specs=[VMEM] * len(args),
        out_specs=VMEM if single else [VMEM] * len(outs),
        compiler_params=pltpu.CompilerParams(vmem_limit_bytes=48 << 20),
    )(*args)


def spread_kernel(cols_ref, wide_ref):
    for at in range(cols_ref.shape[1]):
        wide_ref[at] = jnp.broadcast_to(cols_ref[:, at : at + 1], wide_ref.shape[1:])


def pack_kernel(expand_ref, reduce_ref, hidden_bias_ref, pack_ref, sems):
    units = pack_ref.shape[2]
    moves = []
    for block in range(BLOCKS):
        moves.append((expand_ref.at[block], pack_ref.at[block, pl.ds(0, D)]))
        for part in range(D // units):
            moves.append((
                reduce_ref.at[block, :, pl.ds(units * part, units)],
                pack_ref.at[block, pl.ds(D + units * part, units)],
            ))
    copies = [pltpu.make_async_copy(src, dst, sems.at[i]) for i, (src, dst) in enumerate(moves)]
    for copy in copies:
        copy.start()
    for block in range(BLOCKS):
        rest = hidden_bias_ref[block : block + 1, :]
        pieces = []
        for _ in range(3):
            pieces.append(rest.astype(jnp.bfloat16))
            rest = rest - pieces[-1].astype(jnp.float32)
        pieces = [piece.astype(jnp.float32) for piece in pieces] + [jnp.zeros((5, units), jnp.float32)]
        pack_ref[block, 2 * D :, :] = jnp.concatenate(pieces, axis=0).astype(jnp.bfloat16)
    for copy in copies:
        copy.wait()


def packed(w_expand, w_reduce, hidden_bias):
    units = w_expand.shape[2]
    raw = pl.BlockSpec(memory_space=pl.ANY)
    return pl.pallas_call(
        pack_kernel,
        out_shape=jax.ShapeDtypeStruct((BLOCKS, 2 * D + 8, units), jnp.bfloat16),
        in_specs=[raw, raw, VMEM],
        out_specs=VMEM,
        scratch_shapes=[pltpu.SemaphoreType.DMA((BLOCKS * (1 + D // units),))],
        compiler_params=pltpu.CompilerParams(vmem_limit_bytes=48 << 20),
    )(w_expand, w_reduce, hidden_bias)


def conv_kernel(before_ref, rows_ref, after_ref, wide_ref, out_ref):
    height, share, width = rows_ref.shape
    copies = out_ref.shape[0]
    size = 16
    column = lax.broadcasted_iota(jnp.int32, (size, width), 1)
    inside = {
        shift: ((column + shift >= 0) & (column + shift < width)).astype(jnp.float32)
        for shift in range(-HALF, HALF + 1)
    }
    for group in range(share // size):
        chans = slice(size * group, size * (group + 1))
        rows = [before_ref[r, chans, :] for r in range(height - HALF, height)]
        rows += [rows_ref[r, chans, :] for r in range(height)]
        rows += [after_ref[r, chans, :] for r in range(HALF)]
        rows = [row.astype(jnp.float32) for row in rows]
        totals = [None] * height
        for j in range(TAPS):
            taps = [wide_ref[i * TAPS + j, chans, :] for i in range(TAPS)]
            shift = j - HALF
            for r in range(height):
                acc = rows[r] * taps[0]
                for i in range(1, TAPS):
                    acc = acc + rows[r + i] * taps[i]
                if shift:
                    acc = pltpu.roll(acc, (-shift) % width, 1) * inside[shift]
                totals[r] = acc if totals[r] is None else totals[r] + acc
        for r in range(height):
            half, at = divmod(r, height // CORES)
            value = totals[r].astype(jnp.bfloat16)
            for copy in range(copies):
                out_ref[copy, half, chans, width * at : width * (at + 1)] = value


def mlp_kernel(block, x_ref, gain_ref, bias_ref, expand_ref, reduce_ref, hidden_bias_ref, pack_ref, out_ref):
    x = x_ref[...].reshape(D, x_ref.shape[-1])
    x = jnp.transpose(x).astype(jnp.float32)
    mean = jnp.mean(x, axis=-1, keepdims=True)
    centered = x - mean
    var = jnp.mean(centered * centered, axis=-1, keepdims=True)
    gain = gain_ref[block : block + 1, :]
    bias = bias_ref[block : block + 1, :]
    normed = (centered * lax.rsqrt(var + 1e-06) * gain + bias).astype(jnp.bfloat16)

    def units_of(weights, unit_bias):
        preact = jnp.dot(normed, weights, preferred_element_type=jnp.float32) + unit_bias
        return (0.5 * preact * (1.0 + lax.erf(preact * (0.5**0.5)))).astype(jnp.bfloat16)

    pieces = pack_ref[block, 2 * D :, :].astype(jnp.float32)
    own = units_of(expand_ref[block], hidden_bias_ref[block : block + 1, :])
    other = units_of(pack_ref[block, :D, :], pieces[0:1] + pieces[1:2] + pieces[2:3])
    units = own.shape[1]
    chips, cores, share, half = out_ref.shape
    for part in range(D // units):
        total = jnp.dot(
            own, reduce_ref[block, :, units * part : units * (part + 1)], preferred_element_type=jnp.float32
        ) + jnp.dot(
            other, pack_ref[block, D + units * part : D + units * (part + 1), :], preferred_element_type=jnp.float32
        )
        total = jnp.transpose(total.astype(jnp.bfloat16))
        for at in range(units // share):
            chip, core = divmod(part * (units // share) + at, cores)
            out_ref[chip, core] = total[share * at : share * (at + 1), :]


def mix_kernel(parts_ref, stream_ref, wide_ref, out_ref):
    height, share, width = stream_ref.shape
    scale, shift = wide_ref[TAPS * TAPS], wide_ref[TAPS * TAPS + 1]
    for r in range(height):
        half, at = divmod(r, height // CORES)
        lanes = slice(width * at, width * (at + 1))
        mixed = parts_ref[0, half, :, lanes].astype(jnp.float32)
        for copy in range(1, parts_ref.shape[0]):
            mixed = mixed + parts_ref[copy, half, :, lanes].astype(jnp.float32)
        updated = stream_ref[r].astype(jnp.float32) + scale * (mixed + shift)
        out_ref[r] = updated.astype(jnp.bfloat16)


def per_device(features, depth_kernel, norm_gain, norm_bias, w_expand, b_expand, w_reduce, b_reduce, layer_scale):
    height, width, share = features.shape
    bands, members = lax.axis_size("space"), lax.axis_size("tensor")
    copies = members // CORES
    half = height // CORES * width
    down = [(i, i + 1) for i in range(bands - 1)]
    up = [(j, i) for i, j in down]
    sibling = [(i, i ^ 1) for i in range(members)]

    stream = jnp.transpose(features, (0, 2, 1))
    cols = jnp.concatenate(
        [
            depth_kernel.reshape(BLOCKS, TAPS * TAPS, share).astype(jnp.float32),
            layer_scale[:, None, :],
            b_reduce[:, None, :],
        ],
        axis=1,
    )
    cols = jnp.transpose(cols, (0, 2, 1))

    for block in range(BLOCKS):
        after = lax.ppermute(stream, "space", up)
        before = lax.ppermute(stream, "space", down)
        if block == 0:
            after, cols, own_bias = lax.optimization_barrier((after, cols, b_expand))
            pack = packed(w_expand, w_reduce, own_bias)
        else:
            after, cols = lax.optimization_barrier((after, cols))
        wide = call(
            spread_kernel, jax.ShapeDtypeStruct((TAPS * TAPS + 2, share, width), jnp.float32), cols[block]
        )
        filtered = call(
            conv_kernel,
            jax.ShapeDtypeStruct((copies, CORES, share, half), jnp.bfloat16),
            before, stream, after, wide,
        )
        if block == 0:
            filtered, pack = lax.optimization_barrier((filtered, pack))
            pack = lax.ppermute(pack, "tensor", sibling)
        filtered = lax.all_to_all(filtered.reshape(members, share, half), "tensor", 0, 0, tiled=True)
        partial = call(
            lambda *refs: mlp_kernel(block, *refs),
            jax.ShapeDtypeStruct((copies, CORES, share, half), jnp.bfloat16),
            filtered, norm_gain, norm_bias, w_expand, w_reduce, b_expand, pack,
        )
        partial = lax.all_to_all(partial.reshape(members, share, half), "tensor", 0, 0, tiled=True)
        stream = call(
            mix_kernel,
            jax.ShapeDtypeStruct((height, share, width), jnp.bfloat16),
            partial.reshape(copies, CORES, share, half), stream, wide,
        )
    return jnp.transpose(stream, (0, 2, 1))


def solution(mesh):
    return jax.shard_map(
        per_device,
        mesh=mesh,
        in_specs=(
            P("space", None, "tensor"),
            P(None, None, None, "tensor"),
            P(),
            P(),
            P(None, None, "tensor"),
            P(None, "tensor"),
            P(None, "tensor", None),
            P(None, "tensor"),
            P(None, "tensor"),
        ),
        out_specs=P("space", None, "tensor"),
        check_vma=False,
    )
```

```python
import jax
import jax.numpy as jnp
from jax import lax
from jax.experimental import pallas as pl
from jax.experimental.pallas import tpu as pltpu
from jax.sharding import PartitionSpec as P

D = 1024
TAPS = 7
HALF = TAPS // 2
BLOCKS = 2
CORES = 2

VMEM = pl.BlockSpec(memory_space=pltpu.VMEM)


def call(body, outs, *args, cost=None):
    single = not isinstance(outs, (list, tuple))
    return pl.pallas_call(
        body,
        out_shape=outs,
        in_specs=[VMEM] * len(args),
        out_specs=VMEM if single else [VMEM] * len(outs),
        cost_estimate=cost,
        compiler_params=pltpu.CompilerParams(vmem_limit_bytes=48 << 20),
    )(*args)


def spread_kernel(block, taps_ref, scale_ref, shift_ref, wide_ref):
    rows = [taps_ref[:, block, :].astype(jnp.float32), scale_ref[block : block + 1, :], shift_ref[block : block + 1, :]]
    cols = jnp.transpose(jnp.concatenate(rows, axis=0))
    for at in range(cols.shape[1]):
        wide_ref[at] = jnp.broadcast_to(cols[:, at : at + 1], wide_ref.shape[1:])


def pack_kernel(block, expand_ref, reduce_ref, bias_ref, pack_ref, held_ref, sems):
    units = pack_ref.shape[1]
    moves = [(expand_ref.at[block], pack_ref.at[pl.ds(0, D)])]
    for part in range(D // units):
        columns = pl.ds(units * part, units)
        moves.append((reduce_ref.at[block, :, columns], pack_ref.at[pl.ds(D + units * part, units)]))
    moves.append((bias_ref, held_ref))
    copies = [pltpu.make_async_copy(src, dst, sems.at[i]) for i, (src, dst) in enumerate(moves)]
    for copy in reversed(copies):
        copy.start()
    copies.pop().wait()
    rest = held_ref[block : block + 1, :]
    pieces = []
    for _ in range(3):
        pieces.append(rest.astype(jnp.bfloat16))
        rest = rest - pieces[-1].astype(jnp.float32)
    pieces = [piece.astype(jnp.float32) for piece in pieces] + [jnp.zeros((5, units), jnp.float32)]
    pack_ref[2 * D :, :] = jnp.concatenate(pieces, axis=0).astype(jnp.bfloat16)
    for copy in copies:
        copy.wait()


def packed(block, w_expand, w_reduce, hidden_bias):
    units = w_expand.shape[2]
    raw = pl.BlockSpec(memory_space=pltpu.HBM)
    return pl.pallas_call(
        lambda *refs: pack_kernel(block, *refs),
        out_shape=jax.ShapeDtypeStruct((2 * D + 8, units), jnp.bfloat16),
        in_specs=[raw, raw, raw],
        out_specs=VMEM,
        scratch_shapes=[pltpu.VMEM(hidden_bias.shape, jnp.float32), pltpu.SemaphoreType.DMA((2 + D // units,))],
        compiler_params=pltpu.CompilerParams(vmem_limit_bytes=48 << 20),
    )(*[pltpu.with_memory_space_constraint(array, pltpu.HBM) for array in (w_expand, w_reduce, hidden_bias)])


def conv_kernel(before_ref, rows_ref, after_ref, wide_ref, out_ref):
    height, share, width = rows_ref.shape
    copies = out_ref.shape[0]
    size = 16
    column = lax.broadcasted_iota(jnp.int32, (size, width), 1)
    inside = {
        shift: ((column + shift >= 0) & (column + shift < width)).astype(jnp.float32)
        for shift in range(-HALF, HALF + 1)
    }
    for group in range(share // size):
        chans = slice(size * group, size * (group + 1))
        rows = [before_ref[r, chans, :] for r in range(height - HALF, height)]
        rows += [rows_ref[r, chans, :] for r in range(height)]
        rows += [after_ref[r, chans, :] for r in range(HALF)]
        rows = [row.astype(jnp.float32) for row in rows]
        totals = [None] * height
        for j in range(TAPS):
            taps = [wide_ref[i * TAPS + j, chans, :] for i in range(TAPS)]
            shift = j - HALF
            for r in range(height):
                acc = rows[r] * taps[0]
                for i in range(1, TAPS):
                    acc = acc + rows[r + i] * taps[i]
                if shift:
                    acc = pltpu.roll(acc, (-shift) % width, 1) * inside[shift]
                totals[r] = acc if totals[r] is None else totals[r] + acc
        for r in range(height):
            half, at = divmod(r, height // CORES)
            value = totals[r].astype(jnp.bfloat16)
            for copy in range(copies):
                out_ref[copy, half, chans, width * at : width * (at + 1)] = value


def mlp_kernel(block, x_ref, gain_ref, bias_ref, expand_ref, reduce_ref, hidden_bias_ref, pack_ref, out_ref):
    x = x_ref[...].reshape(D, x_ref.shape[-1])
    x = jnp.transpose(x).astype(jnp.float32)
    mean = jnp.mean(x, axis=-1, keepdims=True)
    centered = x - mean
    var = jnp.mean(centered * centered, axis=-1, keepdims=True)
    gain = gain_ref[block : block + 1, :]
    bias = bias_ref[block : block + 1, :]
    normed = (centered * lax.rsqrt(var + 1e-06) * gain + bias).astype(jnp.bfloat16)

    def units_of(weights, unit_bias):
        preact = jnp.dot(normed, weights, preferred_element_type=jnp.float32) + unit_bias
        return (0.5 * preact * (1.0 + lax.erf(preact * (0.5**0.5)))).astype(jnp.bfloat16)

    pieces = pack_ref[2 * D :, :].astype(jnp.float32)
    own = units_of(expand_ref[block], hidden_bias_ref[block : block + 1, :])
    other = units_of(pack_ref[:D, :], pieces[0:1] + pieces[1:2] + pieces[2:3])
    units = own.shape[1]
    chips, cores, share, half = out_ref.shape
    for part in range(D // units):
        total = jnp.dot(
            own, reduce_ref[block, :, units * part : units * (part + 1)], preferred_element_type=jnp.float32
        ) + jnp.dot(
            other, pack_ref[D + units * part : D + units * (part + 1), :], preferred_element_type=jnp.float32
        )
        total = jnp.transpose(total.astype(jnp.bfloat16))
        for at in range(units // share):
            chip, core = divmod(part * (units // share) + at, cores)
            out_ref[chip, core] = total[share * at : share * (at + 1), :]


def mix_kernel(parts_ref, stream_ref, wide_ref, out_ref):
    height, share, width = stream_ref.shape
    scale, shift = wide_ref[TAPS * TAPS], wide_ref[TAPS * TAPS + 1]
    for r in range(height):
        half, at = divmod(r, height // CORES)
        lanes = slice(width * at, width * (at + 1))
        mixed = parts_ref[0, half, :, lanes].astype(jnp.float32)
        for copy in range(1, parts_ref.shape[0]):
            mixed = mixed + parts_ref[copy, half, :, lanes].astype(jnp.float32)
        updated = stream_ref[r].astype(jnp.float32) + scale * (mixed + shift)
        out_ref[r] = updated.astype(jnp.bfloat16)


def per_device(features, depth_kernel, norm_gain, norm_bias, w_expand, b_expand, w_reduce, b_reduce, layer_scale):
    height, width, share = features.shape
    bands, members = lax.axis_size("space"), lax.axis_size("tensor")
    copies = members // CORES
    half = height // CORES * width
    down = [(i, i + 1) for i in range(bands - 1)]
    up = [(j, i) for i, j in down]
    sibling = [(i, i ^ 1) for i in range(members)]

    stream = jnp.transpose(features, (0, 2, 1))
    taps = jnp.transpose(depth_kernel, (1, 2, 0, 3)).reshape(TAPS * TAPS, BLOCKS, share)

    for block in range(BLOCKS):
        after = lax.ppermute(stream, "space", up)
        before = lax.ppermute(stream, "space", down)
        after, layer_scale, own_bias = lax.optimization_barrier((after, layer_scale, b_expand))
        wide = call(
            lambda *refs: spread_kernel(block, *refs),
            jax.ShapeDtypeStruct((TAPS * TAPS + 2, share, width), jnp.float32),
            taps, layer_scale, b_reduce,
        )
        pack = lax.ppermute(packed(block, w_expand, w_reduce, own_bias), "tensor", sibling)
        filtered = call(
            conv_kernel,
            jax.ShapeDtypeStruct((copies, CORES, share, half), jnp.bfloat16),
            before, stream, after, wide,
            cost=pl.CostEstimate(flops=10**9, transcendentals=0, bytes_accessed=10**6),
        )
        filtered = lax.all_to_all(filtered.reshape(members, share, half), "tensor", 0, 0, tiled=True)
        partial = call(
            lambda *refs: mlp_kernel(block, *refs),
            jax.ShapeDtypeStruct((copies, CORES, share, half), jnp.bfloat16),
            filtered, norm_gain, norm_bias, w_expand, w_reduce, b_expand, pack,
        )
        partial = lax.all_to_all(partial.reshape(members, share, half), "tensor", 0, 0, tiled=True)
        stream = call(
            mix_kernel,
            jax.ShapeDtypeStruct((height, share, width), jnp.bfloat16),
            partial.reshape(copies, CORES, share, half), stream, wide,
        )
    return jnp.transpose(stream, (0, 2, 1))


def solution(mesh):
    return jax.shard_map(
        per_device,
        mesh=mesh,
        in_specs=(
            P("space", None, "tensor"),
            P(None, None, None, "tensor"),
            P(),
            P(),
            P(None, None, "tensor"),
            P(None, "tensor"),
            P(None, "tensor", None),
            P(None, "tensor"),
            P(None, "tensor"),
        ),
        out_specs=P("space", None, "tensor"),
        check_vma=False,
    )
```

```python
import jax
import jax.numpy as jnp
from jax import lax
from jax.experimental import pallas as pl
from jax.experimental.pallas import tpu as pltpu
from jax.sharding import PartitionSpec as P

D = 1024
TAPS = 7
HALF = TAPS // 2
BLOCKS = 2
CORES = 2

VMEM = pl.BlockSpec(memory_space=pltpu.VMEM)


def call(body, outs, *args, cost=None):
    single = not isinstance(outs, (list, tuple))
    return pl.pallas_call(
        body,
        out_shape=outs,
        in_specs=[VMEM] * len(args),
        out_specs=VMEM if single else [VMEM] * len(outs),
        cost_estimate=cost,
        compiler_params=pltpu.CompilerParams(vmem_limit_bytes=16 << 20),
    )(*args)


def spread(block, taps_ref, scale_ref, shift_ref, wide_ref, affine_ref):
    rows = [taps_ref[:, block, :].astype(jnp.float32), scale_ref[block : block + 1, :], shift_ref[block : block + 1, :]]
    cols = jnp.transpose(jnp.concatenate(rows, axis=0))
    for at in range(cols.shape[1]):
        col = jnp.broadcast_to(cols[:, at : at + 1], wide_ref.shape[1:])
        if at < wide_ref.shape[0]:
            wide_ref[at] = col
        else:
            affine_ref[at - wide_ref.shape[0]] = col


def enter_kernel(band_ref, taps_in, scale_in, shift_in, wide_ref, affine_ref, rows_ref, taps_ref, scale_ref, shift_ref, sems):
    moves = ((taps_in, taps_ref), (scale_in, scale_ref), (shift_in, shift_ref), (band_ref, rows_ref))
    copies = [pltpu.make_async_copy(src, dst, sems.at[i]) for i, (src, dst) in enumerate(moves)]
    for copy in copies:
        copy.start()
    for copy in copies[:3]:
        copy.wait()
    spread(0, taps_ref, scale_ref, shift_ref, wide_ref, affine_ref)
    copies[3].wait()


def spread_shapes(share, width):
    return tuple(jax.ShapeDtypeStruct((count, share, width), jnp.float32) for count in (TAPS * TAPS, 2))


def entered(band, taps, scale, shift):
    inputs = (band, taps, scale, shift)
    return pl.pallas_call(
        enter_kernel,
        out_shape=[
            *spread_shapes(*band.shape[1:]),
            *[jax.ShapeDtypeStruct(array.shape, array.dtype) for array in inputs],
        ],
        in_specs=[pl.BlockSpec(memory_space=pltpu.HBM)] * 4,
        out_specs=[VMEM] * 6,
        scratch_shapes=[pltpu.SemaphoreType.DMA((4,))],
        compiler_params=pltpu.CompilerParams(vmem_limit_bytes=16 << 20),
    )(*[pltpu.with_memory_space_constraint(array, pltpu.HBM) for array in inputs])


def pack_kernel(expand_ref, reduce_ref, bias_ref, pack_ref, held_ref, sems):
    units = pack_ref.shape[2]
    moves = []
    for block in range(BLOCKS):
        moves.append((expand_ref.at[block], pack_ref.at[block, pl.ds(0, D)]))
        for part in range(D // units):
            columns = pl.ds(units * part, units)
            moves.append((reduce_ref.at[block, :, columns], pack_ref.at[block, pl.ds(D + units * part, units)]))
    moves.append((bias_ref, held_ref))
    copies = [pltpu.make_async_copy(src, dst, sems.at[i]) for i, (src, dst) in enumerate(moves)]
    for copy in reversed(copies):
        copy.start()
    copies.pop().wait()
    for block in range(BLOCKS):
        rest = held_ref[block : block + 1, :]
        pieces = []
        for _ in range(3):
            pieces.append(rest.astype(jnp.bfloat16))
            rest = rest - pieces[-1].astype(jnp.float32)
        pieces = [piece.astype(jnp.float32) for piece in pieces] + [jnp.zeros((5, units), jnp.float32)]
        pack_ref[block, 2 * D :, :] = jnp.concatenate(pieces, axis=0).astype(jnp.bfloat16)
    for copy in copies:
        copy.wait()


def packed(w_expand, w_reduce, hidden_bias):
    units = w_expand.shape[2]
    raw = pl.BlockSpec(memory_space=pltpu.HBM)
    return pl.pallas_call(
        pack_kernel,
        out_shape=pltpu.VMEM((BLOCKS, 2 * D + 8, units), jnp.bfloat16),
        in_specs=[raw, raw, raw],
        out_specs=VMEM,
        scratch_shapes=[
            pltpu.VMEM(hidden_bias.shape, jnp.float32),
            pltpu.SemaphoreType.DMA((1 + BLOCKS * (1 + D // units),)),
        ],
        compiler_params=pltpu.CompilerParams(vmem_limit_bytes=16 << 20),
    )(*[pltpu.with_memory_space_constraint(array, pltpu.HBM) for array in (w_expand, w_reduce, hidden_bias)])


def conv_kernel(before_ref, rows_ref, after_ref, wide_ref, out_ref):
    height, share, width = rows_ref.shape
    copies = out_ref.shape[0]
    size = 16
    column = lax.broadcasted_iota(jnp.int32, (size, width), 1)
    inside = {
        shift: ((column + shift >= 0) & (column + shift < width)).astype(jnp.float32)
        for shift in range(-HALF, HALF + 1)
    }
    for group in range(share // size):
        chans = slice(size * group, size * (group + 1))
        rows = [before_ref[r, chans, :] for r in range(height - HALF, height)]
        rows += [rows_ref[r, chans, :] for r in range(height)]
        rows += [after_ref[r, chans, :] for r in range(HALF)]
        rows = [row.astype(jnp.float32) for row in rows]
        totals = [None] * height
        for j in range(TAPS):
            taps = [wide_ref[i * TAPS + j, chans, :] for i in range(TAPS)]
            shift = j - HALF
            for r in range(height):
                acc = rows[r] * taps[0]
                for i in range(1, TAPS):
                    acc = acc + rows[r + i] * taps[i]
                if shift:
                    acc = pltpu.roll(acc, (-shift) % width, 1) * inside[shift]
                totals[r] = acc if totals[r] is None else totals[r] + acc
        for r in range(height):
            half, at = divmod(r, height // CORES)
            value = totals[r].astype(jnp.bfloat16)
            for copy in range(copies):
                out_ref[copy, half, chans, width * at : width * (at + 1)] = value


def hidden_of(normed, weights, unit_bias):
    preact = jnp.dot(normed, weights, preferred_element_type=jnp.float32) + unit_bias
    return (0.5 * preact * (1.0 + lax.erf(preact * (0.5**0.5)))).astype(jnp.bfloat16)


def bias_of(rows):
    pieces = rows.astype(jnp.float32)
    return pieces[0:1] + pieces[1:2] + pieces[2:3]


def own_kernel(block, x_ref, gain_ref, bias_ref, pack_ref, normed_ref, own_ref):
    x = x_ref[...].reshape(D, x_ref.shape[-1])
    x = jnp.transpose(x).astype(jnp.float32)
    mean = jnp.mean(x, axis=-1, keepdims=True)
    centered = x - mean
    var = jnp.mean(centered * centered, axis=-1, keepdims=True)
    gain = gain_ref[block : block + 1, :]
    bias = bias_ref[block : block + 1, :]
    normed = (centered * lax.rsqrt(var + 1e-06) * gain + bias).astype(jnp.bfloat16)
    normed_ref[...] = normed
    own_ref[...] = hidden_of(normed, pack_ref[block, :D, :], bias_of(pack_ref[block, 2 * D :, :]))


def rest_kernel(block, normed_ref, own_ref, own_pack_ref, pack_ref, out_ref, held_ref, total_ref, sems):
    bounds = ((0, D), (2 * D, pack_ref.shape[1] - 2 * D), (D, D))
    copies = []
    for i, (start, size) in enumerate(bounds):
        rows = pl.ds(start, size)
        copies.append(pltpu.make_async_copy(pack_ref.at[block, rows], held_ref.at[rows], sems.at[i]))
        copies[-1].start()
    own = own_ref[...]
    units = own.shape[1]
    chips, cores, share, half = out_ref.shape
    for part in range(D // units):
        rows = slice(D + units * part, D + units * (part + 1))
        total_ref[part] = jnp.dot(own, own_pack_ref[block, rows, :], preferred_element_type=jnp.float32)
    copies[0].wait()
    copies[1].wait()
    other = hidden_of(normed_ref[...], held_ref[:D, :], bias_of(held_ref[2 * D :, :]))
    copies[2].wait()
    for part in range(D // units):
        rows = slice(D + units * part, D + units * (part + 1))
        total = total_ref[part] + jnp.dot(other, held_ref[rows, :], preferred_element_type=jnp.float32)
        total = jnp.transpose(total.astype(jnp.bfloat16))
        for at in range(units // share):
            chip, core = divmod(part * (units // share) + at, cores)
            out_ref[chip, core] = total[share * at : share * (at + 1), :]


def rest(block, out, normed, own, own_pack, pack):
    units = own.shape[1]
    return pl.pallas_call(
        lambda *refs: rest_kernel(block, *refs),
        out_shape=out,
        in_specs=[VMEM, VMEM, VMEM, pl.BlockSpec(memory_space=pltpu.HBM)],
        out_specs=VMEM,
        scratch_shapes=[
            pltpu.VMEM(pack.shape[1:], jnp.bfloat16),
            pltpu.VMEM((D // units, own.shape[0], units), jnp.float32),
            pltpu.SemaphoreType.DMA((3,)),
        ],
        compiler_params=pltpu.CompilerParams(vmem_limit_bytes=16 << 20),
    )(normed, own, own_pack, pltpu.with_memory_space_constraint(pack, pltpu.HBM))


def mix_kernel(parts_ref, stream_ref, affine_ref, out_ref):
    height, share, width = stream_ref.shape
    scale, shift = affine_ref[0], affine_ref[1]
    for r in range(height):
        half, at = divmod(r, height // CORES)
        lanes = slice(width * at, width * (at + 1))
        mixed = parts_ref[0, half, :, lanes].astype(jnp.float32)
        for copy in range(1, parts_ref.shape[0]):
            mixed = mixed + parts_ref[copy, half, :, lanes].astype(jnp.float32)
        updated = stream_ref[r].astype(jnp.float32) + scale * (mixed + shift)
        out_ref[r] = updated.astype(jnp.bfloat16)


def per_device(features, depth_kernel, norm_gain, norm_bias, w_expand, b_expand, w_reduce, b_reduce, layer_scale):
    height, width, share = features.shape
    bands, members = lax.axis_size("space"), lax.axis_size("tensor")
    copies = members // CORES
    half = height // CORES * width
    units = w_expand.shape[2]
    down = [(i, i + 1) for i in range(bands - 1)]
    up = [(j, i) for i, j in down]
    sibling = [(i, i ^ 1) for i in range(members)]

    stream = jnp.transpose(features, (0, 2, 1))
    taps = jnp.transpose(depth_kernel, (1, 2, 0, 3)).reshape(TAPS * TAPS, BLOCKS, share)

    for block in range(BLOCKS):
        after = lax.ppermute(stream, "space", up)
        before = lax.ppermute(stream, "space", down)
        if block == 0:
            wide, affine, stream, taps, layer_scale, b_reduce = entered(stream, taps, layer_scale, b_reduce)
        else:
            wide, affine = next_wide, next_affine
        filtered = call(
            conv_kernel,
            jax.ShapeDtypeStruct((copies, CORES, share, half), jnp.bfloat16),
            before, stream, after, wide,
        )
        if block == 0:
            filtered, own_bias, next_scale = lax.optimization_barrier((filtered, b_expand, layer_scale))
            own_pack = packed(w_expand, w_reduce, own_bias)
            pack = lax.ppermute(own_pack, "tensor", sibling)
            next_wide, next_affine = call(
                lambda *refs: spread(1, *refs), spread_shapes(share, width), taps, next_scale, b_reduce
            )
        filtered = lax.all_to_all(filtered.reshape(members, share, half), "tensor", 0, 0, tiled=True)
        if block == 0:
            filtered, next_wide, next_affine = lax.optimization_barrier((filtered, next_wide, next_affine))
        normed, own = call(
            lambda *refs: own_kernel(block, *refs),
            (jax.ShapeDtypeStruct((half, D), jnp.bfloat16), jax.ShapeDtypeStruct((half, units), jnp.bfloat16)),
            filtered, norm_gain, norm_bias, own_pack,
            cost=pl.CostEstimate(flops=10**11, transcendentals=0, bytes_accessed=10**6),
        )
        partial = rest(
            block, jax.ShapeDtypeStruct((copies, CORES, share, half), jnp.bfloat16), normed, own, own_pack, pack
        )
        partial = lax.all_to_all(partial.reshape(members, share, half), "tensor", 0, 0, tiled=True)
        stream = call(
            mix_kernel,
            jax.ShapeDtypeStruct((height, share, width), jnp.bfloat16),
            partial.reshape(copies, CORES, share, half), stream, affine,
        )
    return jnp.transpose(stream, (0, 2, 1))


def solution(mesh):
    return jax.shard_map(
        per_device,
        mesh=mesh,
        in_specs=(
            P("space", None, "tensor"),
            P(None, None, None, "tensor"),
            P(),
            P(),
            P(None, None, "tensor"),
            P(None, "tensor"),
            P(None, "tensor", None),
            P(None, "tensor"),
            P(None, "tensor"),
        ),
        out_specs=P("space", None, "tensor"),
        check_vma=False,
    )
```

```python
import jax
import jax.numpy as jnp
from jax import lax
from jax.experimental import pallas as pl
from jax.experimental.pallas import tpu as pltpu
from jax.sharding import PartitionSpec as P

D = 1024
TAPS = 7
HALF = TAPS // 2
BLOCKS = 2
CHUNKS = 8
CORES = 2

VMEM = pl.BlockSpec(memory_space=pltpu.VMEM)


def call(body, outs, *args, cost=None):
    single = not isinstance(outs, (list, tuple))
    return pl.pallas_call(
        body,
        out_shape=outs,
        in_specs=[VMEM] * len(args),
        out_specs=VMEM if single else [VMEM] * len(outs),
        cost_estimate=cost,
        compiler_params=pltpu.CompilerParams(vmem_limit_bytes=16 << 20),
    )(*args)


def spread(block, taps_ref, scale_ref, shift_ref, wide_ref, affine_ref):
    rows = [taps_ref[:, block, :].astype(jnp.float32), scale_ref[block : block + 1, :], shift_ref[block : block + 1, :]]
    cols = jnp.transpose(jnp.concatenate(rows, axis=0))
    for at in range(cols.shape[1]):
        col = jnp.broadcast_to(cols[:, at : at + 1], wide_ref.shape[1:])
        if at < wide_ref.shape[0]:
            wide_ref[at] = col
        else:
            affine_ref[at - wide_ref.shape[0]] = col


def enter_kernel(band_ref, taps_in, scale_in, shift_in, wide_ref, affine_ref, rows_ref, taps_ref, scale_ref, shift_ref, sems):
    moves = ((taps_in, taps_ref), (scale_in, scale_ref), (shift_in, shift_ref), (band_ref, rows_ref))
    copies = [pltpu.make_async_copy(src, dst, sems.at[i]) for i, (src, dst) in enumerate(moves)]
    for copy in copies:
        copy.start()
    for copy in copies[:3]:
        copy.wait()
    spread(0, taps_ref, scale_ref, shift_ref, wide_ref, affine_ref)
    copies[3].wait()


def spread_shapes(share, width):
    return tuple(jax.ShapeDtypeStruct((count, share, width), jnp.float32) for count in (TAPS * TAPS, 2))


def entered(band, taps, scale, shift):
    inputs = (band, taps, scale, shift)
    return pl.pallas_call(
        enter_kernel,
        out_shape=[
            *spread_shapes(*band.shape[1:]),
            *[jax.ShapeDtypeStruct(array.shape, array.dtype) for array in inputs],
        ],
        in_specs=[pl.BlockSpec(memory_space=pltpu.HBM)] * 4,
        out_specs=[VMEM] * 6,
        scratch_shapes=[pltpu.SemaphoreType.DMA((4,))],
        compiler_params=pltpu.CompilerParams(vmem_limit_bytes=16 << 20),
    )(*[pltpu.with_memory_space_constraint(array, pltpu.HBM) for array in inputs])


def pack_kernel(expand_ref, reduce_ref, bias_ref, pack_ref, held_ref, sems):
    units = pack_ref.shape[2]
    moves = []
    for block in range(BLOCKS):
        ref = pack_ref.at[block]
        moves.append((expand_ref.at[block], ref.at[pl.ds(0, D)]))
        for part in range(D // units):
            columns = pl.ds(units * part, units)
            moves.append((reduce_ref.at[block, :, columns], ref.at[pl.ds(D + units * part, units)]))
    moves.append((bias_ref, held_ref))
    copies = [pltpu.make_async_copy(src, dst, sems.at[i]) for i, (src, dst) in enumerate(moves)]
    for copy in reversed(copies):
        copy.start()
    copies.pop().wait()
    for block in range(BLOCKS):
        rest = held_ref[block : block + 1, :]
        pieces = []
        for _ in range(3):
            pieces.append(rest.astype(jnp.bfloat16))
            rest = rest - pieces[-1].astype(jnp.float32)
        pieces = [piece.astype(jnp.float32) for piece in pieces] + [jnp.zeros((5, units), jnp.float32)]
        pack_ref[block, 2 * D :, :] = jnp.concatenate(pieces, axis=0).astype(jnp.bfloat16)
    for copy in copies:
        copy.wait()


def packed(w_expand, w_reduce, hidden_bias):
    units = w_expand.shape[2]
    raw = pl.BlockSpec(memory_space=pltpu.HBM)
    return pl.pallas_call(
        pack_kernel,
        out_shape=jax.ShapeDtypeStruct((BLOCKS, 2 * D + 8, units), jnp.bfloat16),
        in_specs=[raw, raw, raw],
        out_specs=VMEM,
        scratch_shapes=[
            pltpu.VMEM(hidden_bias.shape, jnp.float32),
            pltpu.SemaphoreType.DMA((1 + BLOCKS * (1 + D // units),)),
        ],
        compiler_params=pltpu.CompilerParams(vmem_limit_bytes=16 << 20),
    )(*[pltpu.with_memory_space_constraint(array, pltpu.HBM) for array in (w_expand, w_reduce, hidden_bias)])


def conv_kernel(before_leads, before_ref, rows_ref, after_ref, wide_ref, out_ref):
    if not before_leads:
        before_ref, after_ref = after_ref, before_ref
    height, share, width = rows_ref.shape
    copies = out_ref.shape[0]
    size = 16
    column = lax.broadcasted_iota(jnp.int32, (size, width), 1)
    inside = {
        shift: ((column + shift >= 0) & (column + shift < width)).astype(jnp.float32)
        for shift in range(-HALF, HALF + 1)
    }
    for group in range(share // size):
        chans = slice(size * group, size * (group + 1))
        rows = [before_ref[r, chans, :] for r in range(before_ref.shape[0] - HALF, before_ref.shape[0])]
        rows += [rows_ref[r, chans, :] for r in range(height)]
        rows += [after_ref[r, chans, :] for r in range(HALF)]
        rows = [row.astype(jnp.float32) for row in rows]
        totals = [None] * height
        for j in range(TAPS):
            taps = [wide_ref[i * TAPS + j, chans, :] for i in range(TAPS)]
            shift = j - HALF
            for r in range(height):
                acc = rows[r] * taps[0]
                for i in range(1, TAPS):
                    acc = acc + rows[r + i] * taps[i]
                if shift:
                    acc = pltpu.roll(acc, (-shift) % width, 1) * inside[shift]
                totals[r] = acc if totals[r] is None else totals[r] + acc
        for r in range(height):
            half, at = divmod(r, height // CORES)
            value = totals[r].astype(jnp.bfloat16)
            for copy in range(copies):
                out_ref[copy, half, chans, width * at : width * (at + 1)] = value


def hidden_of(normed, weights, unit_bias):
    preact = jnp.dot(normed, weights, preferred_element_type=jnp.float32) + unit_bias
    return (0.5 * preact * (1.0 + lax.erf(preact * (0.5**0.5)))).astype(jnp.bfloat16)


def bias_of(rows):
    pieces = rows.astype(jnp.float32)
    return pieces[0:1] + pieces[1:2] + pieces[2:3]


def normalized(block, x_ref, gain_ref, bias_ref):
    x = x_ref[...].reshape(D, x_ref.shape[-1])
    x = jnp.transpose(x).astype(jnp.float32)
    mean = jnp.mean(x, axis=-1, keepdims=True)
    centered = x - mean
    var = jnp.mean(centered * centered, axis=-1, keepdims=True)
    gain = gain_ref[block : block + 1, :]
    bias = bias_ref[block : block + 1, :]
    return (centered * lax.rsqrt(var + 1e-06) * gain + bias).astype(jnp.bfloat16)


def scatter(part, total, out_ref):
    cores, share = out_ref.shape[1:3]
    total = jnp.transpose(total.astype(jnp.bfloat16))
    count = total.shape[0] // share
    for at in range(count):
        chip, core = divmod(part * count + at, cores)
        out_ref[chip, core] = total[share * at : share * (at + 1), :]


def rows_of(part, units):
    return slice(D + units * part, D + units * (part + 1))


def own_kernel(
    block, x_ref, gain_ref, bias_ref, unit_bias_ref, expand_in, reduce_in,
    normed_ref, total_ref, expand_ref, reduce_ref, sems,
):
    parts, half, units = total_ref.shape
    copies = []
    for i in range(2 * CHUNKS):
        src, dst = ((expand_in, expand_ref), (reduce_in, reduce_ref))[i // CHUNKS]
        size = dst.shape[0] // CHUNKS
        rows = pl.ds(size * (i % CHUNKS), size)
        copies.append(pltpu.make_async_copy(src.at[block, rows], dst.at[rows], sems.at[i]))
        copies[-1].start()
    normed = normalized(block, x_ref, gain_ref, bias_ref)
    normed_ref[...] = normed
    for copy in copies[:CHUNKS]:
        copy.wait()
    hidden = hidden_of(normed, expand_ref[...], unit_bias_ref[block : block + 1, :])
    for copy in copies[CHUNKS:]:
        copy.wait()
    for part in range(parts):
        weights = reduce_ref[:, units * part : units * (part + 1)]
        total_ref[part] = jnp.dot(hidden, weights, preferred_element_type=jnp.float32)


def own_part(block, x, gain, bias, unit_bias, w_expand, w_reduce):
    units, half = w_expand.shape[2], x.shape[2]
    raw = pl.BlockSpec(memory_space=pltpu.HBM)
    return pl.pallas_call(
        lambda *refs: own_kernel(block, *refs),
        out_shape=[
            jax.ShapeDtypeStruct((half, D), jnp.bfloat16),
            jax.ShapeDtypeStruct((D // units, half, units), jnp.float32),
        ],
        in_specs=[VMEM, VMEM, VMEM, VMEM, raw, raw],
        out_specs=[VMEM, VMEM],
        scratch_shapes=[
            pltpu.VMEM(w_expand.shape[1:], jnp.bfloat16),
            pltpu.VMEM(w_reduce.shape[1:], jnp.bfloat16),
            pltpu.SemaphoreType.DMA((2 * CHUNKS,)),
        ],
        compiler_params=pltpu.CompilerParams(vmem_limit_bytes=16 << 20),
        cost_estimate=pl.CostEstimate(flops=10**11, transcendentals=0, bytes_accessed=10**6),
    )(x, gain, bias, unit_bias, *[pltpu.with_memory_space_constraint(array, pltpu.HBM) for array in (w_expand, w_reduce)])


def rest_kernel(block, normed_ref, total_ref, pack_ref, out_ref):
    other = hidden_of(normed_ref[...], pack_ref[block, :D, :], bias_of(pack_ref[block, 2 * D :, :]))
    for part in range(total_ref.shape[0]):
        weights = pack_ref[block, rows_of(part, other.shape[1]), :]
        scatter(part, total_ref[part] + jnp.dot(other, weights, preferred_element_type=jnp.float32), out_ref)


def mlp_kernel(block, x_ref, gain_ref, bias_ref, expand_ref, reduce_ref, unit_bias_ref, pack_ref, out_ref):
    normed = normalized(block, x_ref, gain_ref, bias_ref)
    own = hidden_of(normed, expand_ref[block], unit_bias_ref[block : block + 1, :])
    other = hidden_of(normed, pack_ref[block, :D, :], bias_of(pack_ref[block, 2 * D :, :]))
    units = own.shape[1]
    for part in range(D // units):
        own_weights = reduce_ref[block, :, units * part : units * (part + 1)]
        total = jnp.dot(own, own_weights, preferred_element_type=jnp.float32) + jnp.dot(
            other, pack_ref[block, rows_of(part, units), :], preferred_element_type=jnp.float32
        )
        scatter(part, total, out_ref)


def mix_kernel(parts_ref, stream_ref, affine_ref, out_ref, *edge_refs):
    height, share, width = stream_ref.shape
    scale, shift = affine_ref[0], affine_ref[1]
    for r in range(height):
        half, at = divmod(r, height // CORES)
        lanes = slice(width * at, width * (at + 1))
        mixed = parts_ref[0, half, :, lanes].astype(jnp.float32)
        for copy in range(1, parts_ref.shape[0]):
            mixed = mixed + parts_ref[copy, half, :, lanes].astype(jnp.float32)
        updated = stream_ref[r].astype(jnp.float32) + scale * (mixed + shift)
        row = updated.astype(jnp.bfloat16)
        out_ref[r] = row
        for ref, start in zip(edge_refs, (height - HALF, 0)):
            if start <= r < start + HALF:
                ref[r - start] = row


def per_device(features, depth_kernel, norm_gain, norm_bias, w_expand, b_expand, w_reduce, b_reduce, layer_scale):
    height, width, share = features.shape
    bands, members = lax.axis_size("space"), lax.axis_size("tensor")
    copies = members // CORES
    half = height // CORES * width
    units = w_expand.shape[2]
    down = [(i, i + 1) for i in range(bands - 1)]
    up = [(j, i) for i, j in down]
    sibling = [(i, i ^ 1) for i in range(members)]

    stream = jnp.transpose(features, (0, 2, 1))
    taps = jnp.transpose(depth_kernel, (1, 2, 0, 3)).reshape(TAPS * TAPS, BLOCKS, share)

    last = first = stream
    for block in range(BLOCKS):
        before = lax.ppermute(last, "space", down)
        after = lax.ppermute(first, "space", up)
        if block == 0:
            wide, affine, stream, taps, layer_scale, b_reduce = entered(stream, taps, layer_scale, b_reduce)
        else:
            wide, affine = next_wide, next_affine
        edges = (after, before) if block == 0 else (before, after)
        filtered = call(
            lambda *refs: conv_kernel(block > 0, *refs),
            jax.ShapeDtypeStruct((copies, CORES, share, half), jnp.bfloat16),
            edges[0], stream, edges[1], wide,
        )
        if block == 0:
            filtered, own_bias, next_scale = lax.optimization_barrier((filtered, b_expand, layer_scale))
            pack = lax.ppermute(packed(w_expand, w_reduce, own_bias), "tensor", sibling)
            next_wide, next_affine = call(
                lambda *refs: spread(1, *refs), spread_shapes(share, width), taps, next_scale, b_reduce
            )
        filtered = lax.all_to_all(filtered.reshape(members, share, half), "tensor", 0, 0, tiled=True)
        out = jax.ShapeDtypeStruct((copies, CORES, share, half), jnp.bfloat16)
        if block == 0:
            filtered, next_wide, next_affine = lax.optimization_barrier((filtered, next_wide, next_affine))
            normed, total = own_part(block, filtered, norm_gain, norm_bias, b_expand, w_expand, w_reduce)
            partial = call(lambda *refs: rest_kernel(block, *refs), out, normed, total, pack)
        else:
            partial = call(
                lambda *refs: mlp_kernel(block, *refs),
                out,
                filtered, norm_gain, norm_bias, w_expand, w_reduce, b_expand, pack,
            )
        partial = lax.all_to_all(partial.reshape(members, share, half), "tensor", 0, 0, tiled=True)
        partial = partial.reshape(copies, CORES, share, half)
        whole = jax.ShapeDtypeStruct((height, share, width), jnp.bfloat16)
        if block + 1 < BLOCKS:
            edge = jax.ShapeDtypeStruct((HALF, share, width), jnp.bfloat16)
            stream, last, first = call(mix_kernel, (whole, edge, edge), partial, stream, affine)
        else:
            stream = call(mix_kernel, whole, partial, stream, affine)
    return jnp.transpose(stream, (0, 2, 1))


def solution(mesh):
    return jax.shard_map(
        per_device,
        mesh=mesh,
        in_specs=(
            P("space", None, "tensor"),
            P(None, None, None, "tensor"),
            P(),
            P(),
            P(None, None, "tensor"),
            P(None, "tensor"),
            P(None, "tensor", None),
            P(None, "tensor"),
            P(None, "tensor"),
        ),
        out_specs=P("space", None, "tensor"),
        check_vma=False,
    )
```

```python
import jax
import jax.numpy as jnp
from jax import lax
from jax.experimental import pallas as pl
from jax.experimental.pallas import tpu as pltpu
from jax.sharding import PartitionSpec as P

D = 1024
TAPS = 7
HALF = TAPS // 2
BLOCKS = 2
CORES = 2

VMEM = pl.BlockSpec(memory_space=pltpu.VMEM)


def call(body, outs, *args, cost=None):
    single = not isinstance(outs, (list, tuple))
    return pl.pallas_call(
        body,
        out_shape=outs,
        in_specs=[VMEM] * len(args),
        out_specs=VMEM if single else [VMEM] * len(outs),
        cost_estimate=cost,
        compiler_params=pltpu.CompilerParams(vmem_limit_bytes=16 << 20),
    )(*args)


def spread(block, taps_ref, scale_ref, shift_ref, wide_ref, affine_ref):
    rows = [taps_ref[:, block, :].astype(jnp.float32), scale_ref[block : block + 1, :], shift_ref[block : block + 1, :]]
    cols = jnp.transpose(jnp.concatenate(rows, axis=0))
    for at in range(cols.shape[1]):
        col = jnp.broadcast_to(cols[:, at : at + 1], wide_ref.shape[1:])
        if at < wide_ref.shape[0]:
            wide_ref[at] = col
        else:
            affine_ref[at - wide_ref.shape[0]] = col


def enter_kernel(band_ref, taps_in, scale_in, shift_in, wide_ref, affine_ref, rows_ref, taps_ref, scale_ref, shift_ref, sems):
    moves = ((taps_in, taps_ref), (scale_in, scale_ref), (shift_in, shift_ref), (band_ref, rows_ref))
    copies = [pltpu.make_async_copy(src, dst, sems.at[i]) for i, (src, dst) in enumerate(moves)]
    for copy in copies:
        copy.start()
    for copy in copies[:3]:
        copy.wait()
    spread(0, taps_ref, scale_ref, shift_ref, wide_ref, affine_ref)
    copies[3].wait()


def spread_shapes(share, width):
    return tuple(jax.ShapeDtypeStruct((count, share, width), jnp.float32) for count in (TAPS * TAPS, 2))


def entered(band, taps, scale, shift):
    inputs = (band, taps, scale, shift)
    return pl.pallas_call(
        enter_kernel,
        out_shape=[
            *spread_shapes(*band.shape[1:]),
            *[jax.ShapeDtypeStruct(array.shape, array.dtype) for array in inputs],
        ],
        in_specs=[pl.BlockSpec(memory_space=pltpu.HBM)] * 4,
        out_specs=[VMEM] * 6,
        scratch_shapes=[pltpu.SemaphoreType.DMA((4,))],
        compiler_params=pltpu.CompilerParams(vmem_limit_bytes=16 << 20),
    )(*[pltpu.with_memory_space_constraint(array, pltpu.HBM) for array in inputs])


def pack_kernel(expand_ref, reduce_ref, bias_ref, pack_ref, held_ref, sems):
    units = pack_ref.shape[2]
    moves = []
    for block in range(BLOCKS):
        ref = pack_ref.at[block]
        moves.append((expand_ref.at[block], ref.at[pl.ds(0, D)]))
        for part in range(D // units):
            columns = pl.ds(units * part, units)
            moves.append((reduce_ref.at[block, :, columns], ref.at[pl.ds(D + units * part, units)]))
    moves.append((bias_ref, held_ref))
    copies = [pltpu.make_async_copy(src, dst, sems.at[i]) for i, (src, dst) in enumerate(moves)]
    for copy in reversed(copies):
        copy.start()
    copies.pop().wait()
    for block in range(BLOCKS):
        rest = held_ref[block : block + 1, :]
        pieces = []
        for _ in range(3):
            pieces.append(rest.astype(jnp.bfloat16))
            rest = rest - pieces[-1].astype(jnp.float32)
        pieces = [piece.astype(jnp.float32) for piece in pieces] + [jnp.zeros((5, units), jnp.float32)]
        pack_ref[block, 2 * D :, :] = jnp.concatenate(pieces, axis=0).astype(jnp.bfloat16)
    for copy in copies:
        copy.wait()


def packed(w_expand, w_reduce, hidden_bias):
    units = w_expand.shape[2]
    raw = pl.BlockSpec(memory_space=pltpu.HBM)
    return pl.pallas_call(
        pack_kernel,
        out_shape=jax.ShapeDtypeStruct((BLOCKS, 2 * D + 8, units), jnp.bfloat16),
        in_specs=[raw, raw, raw],
        out_specs=VMEM,
        scratch_shapes=[
            pltpu.VMEM(hidden_bias.shape, jnp.float32),
            pltpu.SemaphoreType.DMA((1 + BLOCKS * (1 + D // units),)),
        ],
        compiler_params=pltpu.CompilerParams(vmem_limit_bytes=16 << 20),
    )(*[pltpu.with_memory_space_constraint(array, pltpu.HBM) for array in (w_expand, w_reduce, hidden_bias)])


def conv_kernel(before_leads, before_ref, rows_ref, after_ref, wide_ref, out_ref):
    if not before_leads:
        before_ref, after_ref = after_ref, before_ref
    height, share, width = rows_ref.shape
    copies = out_ref.shape[0]
    size = 16
    column = lax.broadcasted_iota(jnp.int32, (size, width), 1)
    inside = {
        shift: ((column + shift >= 0) & (column + shift < width)).astype(jnp.float32)
        for shift in range(-HALF, HALF + 1)
    }
    for group in range(share // size):
        chans = slice(size * group, size * (group + 1))
        rows = [before_ref[r, chans, :] for r in range(before_ref.shape[0] - HALF, before_ref.shape[0])]
        rows += [rows_ref[r, chans, :] for r in range(height)]
        rows += [after_ref[r, chans, :] for r in range(HALF)]
        rows = [row.astype(jnp.float32) for row in rows]
        totals = [None] * height
        for j in range(TAPS):
            taps = [wide_ref[i * TAPS + j, chans, :] for i in range(TAPS)]
            shift = j - HALF
            for r in range(height):
                acc = rows[r] * taps[0]
                for i in range(1, TAPS):
                    acc = acc + rows[r + i] * taps[i]
                if shift:
                    acc = pltpu.roll(acc, (-shift) % width, 1) * inside[shift]
                totals[r] = acc if totals[r] is None else totals[r] + acc
        for r in range(height):
            half, at = divmod(r, height // CORES)
            value = totals[r].astype(jnp.bfloat16)
            for copy in range(copies):
                out_ref[copy, half, chans, width * at : width * (at + 1)] = value


def hidden_of(normed, weights, unit_bias):
    preact = jnp.dot(normed, weights, preferred_element_type=jnp.float32) + unit_bias
    return (0.5 * preact * (1.0 + lax.erf(preact * (0.5**0.5)))).astype(jnp.bfloat16)


def bias_of(rows):
    pieces = rows.astype(jnp.float32)
    return pieces[0:1] + pieces[1:2] + pieces[2:3]


def normalized(block, x_ref, gain_ref, bias_ref):
    x = x_ref[...].reshape(D, x_ref.shape[-1])
    x = jnp.transpose(x).astype(jnp.float32)
    mean = jnp.mean(x, axis=-1, keepdims=True)
    centered = x - mean
    var = jnp.mean(centered * centered, axis=-1, keepdims=True)
    gain = gain_ref[block : block + 1, :]
    bias = bias_ref[block : block + 1, :]
    return (centered * lax.rsqrt(var + 1e-06) * gain + bias).astype(jnp.bfloat16)


def scatter(part, total, out_ref):
    cores, share = out_ref.shape[1:3]
    total = jnp.transpose(total.astype(jnp.bfloat16))
    count = total.shape[0] // share
    for at in range(count):
        chip, core = divmod(part * count + at, cores)
        out_ref[chip, core] = total[share * at : share * (at + 1), :]


def rows_of(part, units):
    return slice(D + units * part, D + units * (part + 1))


def own_kernel(block, x_ref, gain_ref, bias_ref, unit_bias_ref, expand_ref, normed_ref, own_ref):
    normed = normalized(block, x_ref, gain_ref, bias_ref)
    normed_ref[...] = normed
    own_ref[...] = hidden_of(normed, expand_ref[block], unit_bias_ref[block : block + 1, :])


def rest_kernel(block, normed_ref, own_ref, reduce_ref, pack_ref, out_ref):
    own = own_ref[...]
    units = own.shape[1]
    other = hidden_of(normed_ref[...], pack_ref[block, :D, :], bias_of(pack_ref[block, 2 * D :, :]))
    for part in range(D // units):
        own_weights = reduce_ref[block, :, units * part : units * (part + 1)]
        total = jnp.dot(own, own_weights, preferred_element_type=jnp.float32) + jnp.dot(
            other, pack_ref[block, rows_of(part, units), :], preferred_element_type=jnp.float32
        )
        scatter(part, total, out_ref)


def mlp_kernel(block, x_ref, gain_ref, bias_ref, expand_ref, reduce_ref, unit_bias_ref, pack_ref, out_ref):
    normed = normalized(block, x_ref, gain_ref, bias_ref)
    own = hidden_of(normed, expand_ref[block], unit_bias_ref[block : block + 1, :])
    other = hidden_of(normed, pack_ref[block, :D, :], bias_of(pack_ref[block, 2 * D :, :]))
    units = own.shape[1]
    for part in range(D // units):
        own_weights = reduce_ref[block, :, units * part : units * (part + 1)]
        total = jnp.dot(own, own_weights, preferred_element_type=jnp.float32) + jnp.dot(
            other, pack_ref[block, rows_of(part, units), :], preferred_element_type=jnp.float32
        )
        scatter(part, total, out_ref)


def mix_kernel(parts_ref, stream_ref, affine_ref, out_ref, *edge_refs):
    height, share, width = stream_ref.shape
    scale, shift = affine_ref[0], affine_ref[1]
    for r in range(height):
        half, at = divmod(r, height // CORES)
        lanes = slice(width * at, width * (at + 1))
        mixed = parts_ref[0, half, :, lanes].astype(jnp.float32)
        for copy in range(1, parts_ref.shape[0]):
            mixed = mixed + parts_ref[copy, half, :, lanes].astype(jnp.float32)
        updated = stream_ref[r].astype(jnp.float32) + scale * (mixed + shift)
        row = updated.astype(jnp.bfloat16)
        out_ref[r] = row
        for ref, start in zip(edge_refs, (height - HALF, 0)):
            if start <= r < start + HALF:
                ref[r - start] = row


def per_device(features, depth_kernel, norm_gain, norm_bias, w_expand, b_expand, w_reduce, b_reduce, layer_scale):
    height, width, share = features.shape
    bands, members = lax.axis_size("space"), lax.axis_size("tensor")
    copies = members // CORES
    half = height // CORES * width
    units = w_expand.shape[2]
    down = [(i, i + 1) for i in range(bands - 1)]
    up = [(j, i) for i, j in down]
    sibling = [(i, i ^ 1) for i in range(members)]

    stream = jnp.transpose(features, (0, 2, 1))
    taps = jnp.transpose(depth_kernel, (1, 2, 0, 3)).reshape(TAPS * TAPS, BLOCKS, share)

    last = first = stream
    for block in range(BLOCKS):
        before = lax.ppermute(last, "space", down)
        after = lax.ppermute(first, "space", up)
        if block == 0:
            wide, affine, stream, taps, layer_scale, b_reduce = entered(stream, taps, layer_scale, b_reduce)
        else:
            wide, affine = next_wide, next_affine
        edges = (after, before) if block == 0 else (before, after)
        filtered = call(
            lambda *refs: conv_kernel(block > 0, *refs),
            jax.ShapeDtypeStruct((copies, CORES, share, half), jnp.bfloat16),
            edges[0], stream, edges[1], wide,
        )
        if block == 0:
            filtered, own_bias, next_scale = lax.optimization_barrier((filtered, b_expand, layer_scale))
            pack = lax.ppermute(packed(w_expand, w_reduce, own_bias), "tensor", sibling)
            next_wide, next_affine = call(
                lambda *refs: spread(1, *refs), spread_shapes(share, width), taps, next_scale, b_reduce
            )
        filtered = lax.all_to_all(filtered.reshape(members, share, half), "tensor", 0, 0, tiled=True)
        out = jax.ShapeDtypeStruct((copies, CORES, share, half), jnp.bfloat16)
        if block == 0:
            filtered, next_wide, next_affine = lax.optimization_barrier((filtered, next_wide, next_affine))
            normed, own = call(
                lambda *refs: own_kernel(block, *refs),
                (jax.ShapeDtypeStruct((half, D), jnp.bfloat16), jax.ShapeDtypeStruct((half, units), jnp.bfloat16)),
                filtered, norm_gain, norm_bias, b_expand, w_expand,
                cost=pl.CostEstimate(flops=10**11, transcendentals=0, bytes_accessed=10**6),
            )
            partial = call(lambda *refs: rest_kernel(block, *refs), out, normed, own, w_reduce, pack)
        else:
            partial = call(
                lambda *refs: mlp_kernel(block, *refs),
                out,
                filtered, norm_gain, norm_bias, w_expand, w_reduce, b_expand, pack,
            )
        partial = lax.all_to_all(partial.reshape(members, share, half), "tensor", 0, 0, tiled=True)
        partial = partial.reshape(copies, CORES, share, half)
        whole = jax.ShapeDtypeStruct((height, share, width), jnp.bfloat16)
        if block + 1 < BLOCKS:
            edge = jax.ShapeDtypeStruct((HALF, share, width), jnp.bfloat16)
            stream, last, first = call(mix_kernel, (whole, edge, edge), partial, stream, affine)
        else:
            stream = call(mix_kernel, whole, partial, stream, affine)
    return jnp.transpose(stream, (0, 2, 1))


def solution(mesh):
    return jax.shard_map(
        per_device,
        mesh=mesh,
        in_specs=(
            P("space", None, "tensor"),
            P(None, None, None, "tensor"),
            P(),
            P(),
            P(None, None, "tensor"),
            P(None, "tensor"),
            P(None, "tensor", None),
            P(None, "tensor"),
            P(None, "tensor"),
        ),
        out_specs=P("space", None, "tensor"),
        check_vma=False,
    )
```

```python
import jax
import jax.numpy as jnp
from jax import lax
from jax.experimental import pallas as pl
from jax.experimental.pallas import tpu as pltpu
from jax.sharding import PartitionSpec as P

D = 1024
TAPS = 7
HALF = TAPS // 2
BLOCKS = 2
CORES = 2

VMEM = pl.BlockSpec(memory_space=pltpu.VMEM)


def call(body, outs, *args, cost=None):
    single = not isinstance(outs, (list, tuple))
    return pl.pallas_call(
        body,
        out_shape=outs,
        in_specs=[VMEM] * len(args),
        out_specs=VMEM if single else [VMEM] * len(outs),
        cost_estimate=cost,
        compiler_params=pltpu.CompilerParams(vmem_limit_bytes=16 << 20),
    )(*args)


def spread(block, taps_ref, scale_ref, shift_ref, wide_ref, affine_ref):
    rows = [taps_ref[:, block, :].astype(jnp.float32), scale_ref[block : block + 1, :], shift_ref[block : block + 1, :]]
    cols = jnp.transpose(jnp.concatenate(rows, axis=0))
    for at in range(cols.shape[1]):
        col = jnp.broadcast_to(cols[:, at : at + 1], wide_ref.shape[1:])
        if at < wide_ref.shape[0]:
            wide_ref[at] = col
        else:
            affine_ref[at - wide_ref.shape[0]] = col


def enter_kernel(band_ref, taps_in, scale_in, shift_in, wide_ref, affine_ref, rows_ref, taps_ref, scale_ref, shift_ref, sems):
    moves = ((taps_in, taps_ref), (scale_in, scale_ref), (shift_in, shift_ref), (band_ref, rows_ref))
    copies = [pltpu.make_async_copy(src, dst, sems.at[i]) for i, (src, dst) in enumerate(moves)]
    for copy in copies:
        copy.start()
    for copy in copies[:3]:
        copy.wait()
    spread(0, taps_ref, scale_ref, shift_ref, wide_ref, affine_ref)
    copies[3].wait()


def spread_shapes(share, width):
    return tuple(jax.ShapeDtypeStruct((count, share, width), jnp.float32) for count in (TAPS * TAPS, 2))


def entered(band, taps, scale, shift):
    inputs = (band, taps, scale, shift)
    return pl.pallas_call(
        enter_kernel,
        out_shape=[
            *spread_shapes(*band.shape[1:]),
            *[jax.ShapeDtypeStruct(array.shape, array.dtype) for array in inputs],
        ],
        in_specs=[pl.BlockSpec(memory_space=pltpu.HBM)] * 4,
        out_specs=[VMEM] * 6,
        scratch_shapes=[pltpu.SemaphoreType.DMA((4,))],
        compiler_params=pltpu.CompilerParams(vmem_limit_bytes=16 << 20),
    )(*[pltpu.with_memory_space_constraint(array, pltpu.HBM) for array in inputs])


def pack_kernel(expand_ref, reduce_ref, bias_ref, pack_ref, held_ref, sems):
    units = pack_ref.shape[2]
    moves = []
    for block in range(BLOCKS):
        ref = pack_ref.at[block]
        moves.append((expand_ref.at[block], ref.at[pl.ds(0, D)]))
        for part in range(D // units):
            columns = pl.ds(units * part, units)
            moves.append((reduce_ref.at[block, :, columns], ref.at[pl.ds(D + units * part, units)]))
    moves.append((bias_ref, held_ref))
    copies = [pltpu.make_async_copy(src, dst, sems.at[i]) for i, (src, dst) in enumerate(moves)]
    for copy in reversed(copies):
        copy.start()
    copies.pop().wait()
    for block in range(BLOCKS):
        rest = held_ref[block : block + 1, :]
        pieces = []
        for _ in range(3):
            pieces.append(rest.astype(jnp.bfloat16))
            rest = rest - pieces[-1].astype(jnp.float32)
        pieces = [piece.astype(jnp.float32) for piece in pieces] + [jnp.zeros((5, units), jnp.float32)]
        pack_ref[block, 2 * D :, :] = jnp.concatenate(pieces, axis=0).astype(jnp.bfloat16)
    for copy in copies:
        copy.wait()


def packed(w_expand, w_reduce, hidden_bias):
    units = w_expand.shape[2]
    raw = pl.BlockSpec(memory_space=pltpu.HBM)
    return pl.pallas_call(
        pack_kernel,
        out_shape=jax.ShapeDtypeStruct((BLOCKS, 2 * D + 8, units), jnp.bfloat16),
        in_specs=[raw, raw, raw],
        out_specs=VMEM,
        scratch_shapes=[
            pltpu.VMEM(hidden_bias.shape, jnp.float32),
            pltpu.SemaphoreType.DMA((1 + BLOCKS * (1 + D // units),)),
        ],
        compiler_params=pltpu.CompilerParams(vmem_limit_bytes=16 << 20),
    )(*[pltpu.with_memory_space_constraint(array, pltpu.HBM) for array in (w_expand, w_reduce, hidden_bias)])


def conv_kernel(before_leads, before_ref, rows_ref, after_ref, wide_ref, out_ref):
    if not before_leads:
        before_ref, after_ref = after_ref, before_ref
    height, share, width = rows_ref.shape
    copies = out_ref.shape[0]
    size = 16
    column = lax.broadcasted_iota(jnp.int32, (size, width), 1)
    inside = {
        shift: ((column + shift >= 0) & (column + shift < width)).astype(jnp.float32)
        for shift in range(-HALF, HALF + 1)
    }
    for group in range(share // size):
        chans = slice(size * group, size * (group + 1))
        rows = [before_ref[r, chans, :] for r in range(before_ref.shape[0] - HALF, before_ref.shape[0])]
        rows += [rows_ref[r, chans, :] for r in range(height)]
        rows += [after_ref[r, chans, :] for r in range(HALF)]
        rows = [row.astype(jnp.float32) for row in rows]
        totals = [None] * height
        for j in range(TAPS):
            taps = [wide_ref[i * TAPS + j, chans, :] for i in range(TAPS)]
            shift = j - HALF
            for r in range(height):
                acc = rows[r] * taps[0]
                for i in range(1, TAPS):
                    acc = acc + rows[r + i] * taps[i]
                if shift:
                    acc = pltpu.roll(acc, (-shift) % width, 1) * inside[shift]
                totals[r] = acc if totals[r] is None else totals[r] + acc
        for r in range(height):
            half, at = divmod(r, height // CORES)
            value = totals[r].astype(jnp.bfloat16)
            for copy in range(copies):
                out_ref[copy, half, chans, width * at : width * (at + 1)] = value


def hidden_of(normed, weights, unit_bias):
    preact = jnp.dot(normed, weights, preferred_element_type=jnp.float32) + unit_bias
    return (0.5 * preact * (1.0 + lax.erf(preact * (0.5**0.5)))).astype(jnp.bfloat16)


def bias_of(rows):
    pieces = rows.astype(jnp.float32)
    return pieces[0:1] + pieces[1:2] + pieces[2:3]


def normalized(block, x_ref, gain_ref, bias_ref):
    x = x_ref[...].reshape(D, x_ref.shape[-1])
    x = jnp.transpose(x).astype(jnp.float32)
    mean = jnp.mean(x, axis=-1, keepdims=True)
    centered = x - mean
    var = jnp.mean(centered * centered, axis=-1, keepdims=True)
    gain = gain_ref[block : block + 1, :]
    bias = bias_ref[block : block + 1, :]
    return (centered * lax.rsqrt(var + 1e-06) * gain + bias).astype(jnp.bfloat16)


def scatter(part, total, out_ref):
    cores, share = out_ref.shape[1:3]
    total = jnp.transpose(total.astype(jnp.bfloat16))
    count = total.shape[0] // share
    for at in range(count):
        chip, core = divmod(part * count + at, cores)
        out_ref[chip, core] = total[share * at : share * (at + 1), :]


def rows_of(part, units):
    return slice(D + units * part, D + units * (part + 1))


def mlp_kernel(block, x_ref, gain_ref, bias_ref, expand_ref, reduce_ref, unit_bias_ref, pack_ref, out_ref):
    normed = normalized(block, x_ref, gain_ref, bias_ref)
    own = hidden_of(normed, expand_ref[block], unit_bias_ref[block : block + 1, :])
    other = hidden_of(normed, pack_ref[block, :D, :], bias_of(pack_ref[block, 2 * D :, :]))
    units = own.shape[1]
    for part in range(D // units):
        own_weights = reduce_ref[block, :, units * part : units * (part + 1)]
        total = jnp.dot(own, own_weights, preferred_element_type=jnp.float32) + jnp.dot(
            other, pack_ref[block, rows_of(part, units), :], preferred_element_type=jnp.float32
        )
        scatter(part, total, out_ref)


def mix_kernel(parts_ref, stream_ref, affine_ref, out_ref, *edge_refs):
    height, share, width = stream_ref.shape
    scale, shift = affine_ref[0], affine_ref[1]
    for r in range(height):
        half, at = divmod(r, height // CORES)
        lanes = slice(width * at, width * (at + 1))
        mixed = parts_ref[0, half, :, lanes].astype(jnp.float32)
        for copy in range(1, parts_ref.shape[0]):
            mixed = mixed + parts_ref[copy, half, :, lanes].astype(jnp.float32)
        updated = stream_ref[r].astype(jnp.float32) + scale * (mixed + shift)
        row = updated.astype(jnp.bfloat16)
        out_ref[r] = row
        for ref, start in zip(edge_refs, (height - HALF, 0)):
            if start <= r < start + HALF:
                ref[r - start] = row


def per_device(features, depth_kernel, norm_gain, norm_bias, w_expand, b_expand, w_reduce, b_reduce, layer_scale):
    height, width, share = features.shape
    bands, members = lax.axis_size("space"), lax.axis_size("tensor")
    copies = members // CORES
    half = height // CORES * width
    units = w_expand.shape[2]
    down = [(i, i + 1) for i in range(bands - 1)]
    up = [(j, i) for i, j in down]
    sibling = [(i, i ^ 1) for i in range(members)]

    stream = jnp.transpose(features, (0, 2, 1))
    taps = jnp.transpose(depth_kernel, (1, 2, 0, 3)).reshape(TAPS * TAPS, BLOCKS, share)

    last = first = stream
    for block in range(BLOCKS):
        before = lax.ppermute(last, "space", down)
        after = lax.ppermute(first, "space", up)
        if block == 0:
            wide, affine, stream, taps, layer_scale, b_reduce = entered(stream, taps, layer_scale, b_reduce)
            layer_scale, own_bias = lax.optimization_barrier((layer_scale, b_expand))
            pack = lax.ppermute(packed(w_expand, w_reduce, own_bias), "tensor", sibling)
        else:
            stream, next_scale = lax.optimization_barrier((stream, layer_scale))
            wide, affine = call(
                lambda *refs: spread(1, *refs), spread_shapes(share, width), taps, next_scale, b_reduce
            )
        edges = (after, before) if block == 0 else (before, after)
        filtered = call(
            lambda *refs: conv_kernel(block > 0, *refs),
            jax.ShapeDtypeStruct((copies, CORES, share, half), jnp.bfloat16),
            edges[0], stream, edges[1], wide,
            cost=pl.CostEstimate(flops=10**11, transcendentals=0, bytes_accessed=10**6) if block == 0 else None,
        )
        filtered = lax.all_to_all(filtered.reshape(members, share, half), "tensor", 0, 0, tiled=True)
        out = jax.ShapeDtypeStruct((copies, CORES, share, half), jnp.bfloat16)
        partial = call(
            lambda *refs: mlp_kernel(block, *refs),
            out,
            filtered, norm_gain, norm_bias, w_expand, w_reduce, b_expand, pack,
        )
        partial = lax.all_to_all(partial.reshape(members, share, half), "tensor", 0, 0, tiled=True)
        partial = partial.reshape(copies, CORES, share, half)
        whole = jax.ShapeDtypeStruct((height, share, width), jnp.bfloat16)
        if block + 1 < BLOCKS:
            edge = jax.ShapeDtypeStruct((HALF, share, width), jnp.bfloat16)
            stream, last, first = call(mix_kernel, (whole, edge, edge), partial, stream, affine)
        else:
            stream = call(mix_kernel, whole, partial, stream, affine)
    return jnp.transpose(stream, (0, 2, 1))


def solution(mesh):
    return jax.shard_map(
        per_device,
        mesh=mesh,
        in_specs=(
            P("space", None, "tensor"),
            P(None, None, None, "tensor"),
            P(),
            P(),
            P(None, None, "tensor"),
            P(None, "tensor"),
            P(None, "tensor", None),
            P(None, "tensor"),
            P(None, "tensor"),
        ),
        out_specs=P("space", None, "tensor"),
        check_vma=False,
    )
```

```python
import jax
import jax.numpy as jnp
from jax import lax
from jax.experimental import pallas as pl
from jax.experimental.pallas import tpu as pltpu
from jax.sharding import PartitionSpec as P

D = 1024
TAPS = 7
HALF = TAPS // 2
BLOCKS = 2
CORES = 2

VMEM = pl.BlockSpec(memory_space=pltpu.VMEM)


def call(body, outs, *args, cost=None):
    single = not isinstance(outs, (list, tuple))
    return pl.pallas_call(
        body,
        out_shape=outs,
        in_specs=[VMEM] * len(args),
        out_specs=VMEM if single else [VMEM] * len(outs),
        cost_estimate=cost,
        compiler_params=pltpu.CompilerParams(vmem_limit_bytes=16 << 20),
    )(*args)


def spread(block, taps_ref, scale_ref, shift_ref, wide_ref, affine_ref):
    rows = [taps_ref[:, block, :].astype(jnp.float32), scale_ref[block : block + 1, :], shift_ref[block : block + 1, :]]
    cols = jnp.transpose(jnp.concatenate(rows, axis=0))
    for at in range(cols.shape[1]):
        col = jnp.broadcast_to(cols[:, at : at + 1], wide_ref.shape[1:])
        if at < wide_ref.shape[0]:
            wide_ref[at] = col
        else:
            affine_ref[at - wide_ref.shape[0]] = col


def enter_kernel(
    band_in, taps_in, scale_in, shift_in, expand_in, reduce_in, bias_in,
    wide_ref, affine_ref, rows_ref, taps_ref, scale_ref, shift_ref, pack_ref, held_ref, sems,
):
    units = pack_ref.shape[2]
    moves = [(taps_in, taps_ref), (scale_in, scale_ref), (shift_in, shift_ref), (bias_in, held_ref)]
    small = len(moves)
    for block in range(BLOCKS):
        ref = pack_ref.at[block]
        moves.append((expand_in.at[block], ref.at[pl.ds(0, D)]))
        for part in range(D // units):
            columns = pl.ds(units * part, units)
            moves.append((reduce_in.at[block, :, columns], ref.at[pl.ds(D + units * part, units)]))
    moves.append((band_in, rows_ref))
    copies = [pltpu.make_async_copy(src, dst, sems.at[i]) for i, (src, dst) in enumerate(moves)]
    for copy in copies:
        copy.start()
    for copy in copies[:small]:
        copy.wait()
    spread(0, taps_ref, scale_ref, shift_ref, wide_ref, affine_ref)
    for block in range(BLOCKS):
        rest = held_ref[block : block + 1, :]
        pieces = []
        for _ in range(3):
            pieces.append(rest.astype(jnp.bfloat16))
            rest = rest - pieces[-1].astype(jnp.float32)
        pieces = [piece.astype(jnp.float32) for piece in pieces] + [jnp.zeros((5, units), jnp.float32)]
        pack_ref[block, 2 * D :, :] = jnp.concatenate(pieces, axis=0).astype(jnp.bfloat16)
    for copy in copies[small:]:
        copy.wait()


def spread_shapes(share, width):
    return tuple(jax.ShapeDtypeStruct((count, share, width), jnp.float32) for count in (TAPS * TAPS, 2))


def entered(band, taps, scale, shift, w_expand, w_reduce, b_expand):
    units = w_expand.shape[2]
    inputs = (band, taps, scale, shift, w_expand, w_reduce, b_expand)
    outs = [
        *spread_shapes(*band.shape[1:]),
        *[jax.ShapeDtypeStruct(array.shape, array.dtype) for array in inputs[:4]],
        jax.ShapeDtypeStruct((BLOCKS, 2 * D + 8, units), jnp.bfloat16),
    ]
    return pl.pallas_call(
        enter_kernel,
        out_shape=outs,
        in_specs=[pl.BlockSpec(memory_space=pltpu.HBM)] * len(inputs),
        out_specs=[VMEM] * len(outs),
        scratch_shapes=[
            pltpu.VMEM(b_expand.shape, jnp.float32),
            pltpu.SemaphoreType.DMA((5 + BLOCKS * (1 + D // units),)),
        ],
        compiler_params=pltpu.CompilerParams(vmem_limit_bytes=16 << 20),
    )(*[pltpu.with_memory_space_constraint(array, pltpu.HBM) for array in inputs])


def conv_kernel(before_leads, before_ref, rows_ref, after_ref, wide_ref, out_ref):
    if not before_leads:
        before_ref, after_ref = after_ref, before_ref
    height, share, width = rows_ref.shape
    copies = out_ref.shape[0]
    size = 16
    column = lax.broadcasted_iota(jnp.int32, (size, width), 1)
    inside = {
        shift: ((column + shift >= 0) & (column + shift < width)).astype(jnp.float32)
        for shift in range(-HALF, HALF + 1)
    }
    for group in range(share // size):
        chans = slice(size * group, size * (group + 1))
        rows = [before_ref[r, chans, :] for r in range(before_ref.shape[0] - HALF, before_ref.shape[0])]
        rows += [rows_ref[r, chans, :] for r in range(height)]
        rows += [after_ref[r, chans, :] for r in range(HALF)]
        rows = [row.astype(jnp.float32) for row in rows]
        totals = [None] * height
        for j in range(TAPS):
            taps = [wide_ref[i * TAPS + j, chans, :] for i in range(TAPS)]
            shift = j - HALF
            for r in range(height):
                acc = rows[r] * taps[0]
                for i in range(1, TAPS):
                    acc = acc + rows[r + i] * taps[i]
                if shift:
                    acc = pltpu.roll(acc, (-shift) % width, 1) * inside[shift]
                totals[r] = acc if totals[r] is None else totals[r] + acc
        for r in range(height):
            half, at = divmod(r, height // CORES)
            value = totals[r].astype(jnp.bfloat16)
            for copy in range(copies):
                out_ref[copy, half, chans, width * at : width * (at + 1)] = value


def hidden_of(normed, weights, unit_bias):
    preact = jnp.dot(normed, weights, preferred_element_type=jnp.float32) + unit_bias
    return (0.5 * preact * (1.0 + lax.erf(preact * (0.5**0.5)))).astype(jnp.bfloat16)


def bias_of(rows):
    pieces = rows.astype(jnp.float32)
    return pieces[0:1] + pieces[1:2] + pieces[2:3]


def normalized(block, x_ref, gain_ref, bias_ref):
    x = x_ref[...].reshape(D, x_ref.shape[-1])
    x = jnp.transpose(x).astype(jnp.float32)
    mean = jnp.mean(x, axis=-1, keepdims=True)
    centered = x - mean
    var = jnp.mean(centered * centered, axis=-1, keepdims=True)
    gain = gain_ref[block : block + 1, :]
    bias = bias_ref[block : block + 1, :]
    return (centered * lax.rsqrt(var + 1e-06) * gain + bias).astype(jnp.bfloat16)


def scatter(part, total, out_ref):
    cores, share = out_ref.shape[1:3]
    total = jnp.transpose(total.astype(jnp.bfloat16))
    count = total.shape[0] // share
    for at in range(count):
        chip, core = divmod(part * count + at, cores)
        out_ref[chip, core] = total[share * at : share * (at + 1), :]


def rows_of(part, units):
    return slice(D + units * part, D + units * (part + 1))


def mlp_kernel(block, x_ref, gain_ref, bias_ref, expand_ref, reduce_ref, unit_bias_ref, pack_ref, out_ref):
    normed = normalized(block, x_ref, gain_ref, bias_ref)
    own = hidden_of(normed, expand_ref[block], unit_bias_ref[block : block + 1, :])
    other = hidden_of(normed, pack_ref[block, :D, :], bias_of(pack_ref[block, 2 * D :, :]))
    units = own.shape[1]
    for part in range(D // units):
        own_weights = reduce_ref[block, :, units * part : units * (part + 1)]
        total = jnp.dot(own, own_weights, preferred_element_type=jnp.float32) + jnp.dot(
            other, pack_ref[block, rows_of(part, units), :], preferred_element_type=jnp.float32
        )
        scatter(part, total, out_ref)


def mix_kernel(parts_ref, stream_ref, affine_ref, out_ref, *edge_refs):
    height, share, width = stream_ref.shape
    scale, shift = affine_ref[0], affine_ref[1]
    for r in range(height):
        half, at = divmod(r, height // CORES)
        lanes = slice(width * at, width * (at + 1))
        mixed = parts_ref[0, half, :, lanes].astype(jnp.float32)
        for copy in range(1, parts_ref.shape[0]):
            mixed = mixed + parts_ref[copy, half, :, lanes].astype(jnp.float32)
        updated = stream_ref[r].astype(jnp.float32) + scale * (mixed + shift)
        row = updated.astype(jnp.bfloat16)
        out_ref[r] = row
        for ref, start in zip(edge_refs, (height - HALF, 0)):
            if start <= r < start + HALF:
                ref[r - start] = row


def per_device(features, depth_kernel, norm_gain, norm_bias, w_expand, b_expand, w_reduce, b_reduce, layer_scale):
    height, width, share = features.shape
    bands, members = lax.axis_size("space"), lax.axis_size("tensor")
    copies = members // CORES
    half = height // CORES * width
    units = w_expand.shape[2]
    down = [(i, i + 1) for i in range(bands - 1)]
    up = [(j, i) for i, j in down]
    sibling = [(i, i ^ 1) for i in range(members)]

    stream = jnp.transpose(features, (0, 2, 1))
    taps = jnp.transpose(depth_kernel, (1, 2, 0, 3)).reshape(TAPS * TAPS, BLOCKS, share)

    last = first = stream
    for block in range(BLOCKS):
        before = lax.ppermute(last, "space", down)
        after = lax.ppermute(first, "space", up)
        if block == 0:
            wide, affine, stream, taps, layer_scale, b_reduce, pack = entered(
                stream, taps, layer_scale, b_reduce, w_expand, w_reduce, b_expand
            )
            pack = lax.ppermute(pack, "tensor", sibling)
        else:
            stream, next_scale = lax.optimization_barrier((stream, layer_scale))
            wide, affine = call(
                lambda *refs: spread(1, *refs), spread_shapes(share, width), taps, next_scale, b_reduce
            )
        edges = (after, before) if block == 0 else (before, after)
        filtered = call(
            lambda *refs: conv_kernel(block > 0, *refs),
            jax.ShapeDtypeStruct((copies, CORES, share, half), jnp.bfloat16),
            edges[0], stream, edges[1], wide,
            cost=pl.CostEstimate(flops=10**11, transcendentals=0, bytes_accessed=10**6) if block == 0 else None,
        )
        filtered = lax.all_to_all(filtered.reshape(members, share, half), "tensor", 0, 0, tiled=True)
        out = jax.ShapeDtypeStruct((copies, CORES, share, half), jnp.bfloat16)
        partial = call(
            lambda *refs: mlp_kernel(block, *refs),
            out,
            filtered, norm_gain, norm_bias, w_expand, w_reduce, b_expand, pack,
        )
        partial = lax.all_to_all(partial.reshape(members, share, half), "tensor", 0, 0, tiled=True)
        partial = partial.reshape(copies, CORES, share, half)
        whole = jax.ShapeDtypeStruct((height, share, width), jnp.bfloat16)
        if block + 1 < BLOCKS:
            edge = jax.ShapeDtypeStruct((HALF, share, width), jnp.bfloat16)
            stream, last, first = call(mix_kernel, (whole, edge, edge), partial, stream, affine)
        else:
            stream = call(mix_kernel, whole, partial, stream, affine)
    return jnp.transpose(stream, (0, 2, 1))


def solution(mesh):
    return jax.shard_map(
        per_device,
        mesh=mesh,
        in_specs=(
            P("space", None, "tensor"),
            P(None, None, None, "tensor"),
            P(),
            P(),
            P(None, None, "tensor"),
            P(None, "tensor"),
            P(None, "tensor", None),
            P(None, "tensor"),
            P(None, "tensor"),
        ),
        out_specs=P("space", None, "tensor"),
        check_vma=False,
    )
```

```python
import jax
import jax.numpy as jnp
from jax import lax
from jax.experimental import pallas as pl
from jax.experimental.pallas import tpu as pltpu
from jax.sharding import PartitionSpec as P

D = 1024
TAPS = 7
HALF = TAPS // 2
BLOCKS = 2
CORES = 2

VMEM = pl.BlockSpec(memory_space=pltpu.VMEM)


def call(body, outs, *args, cost=None):
    single = not isinstance(outs, (list, tuple))
    return pl.pallas_call(
        body,
        out_shape=outs,
        in_specs=[VMEM] * len(args),
        out_specs=VMEM if single else [VMEM] * len(outs),
        cost_estimate=cost,
        compiler_params=pltpu.CompilerParams(vmem_limit_bytes=16 << 20),
    )(*args)


def spread(block, taps_ref, scale_ref, shift_ref, wide_ref, affine_ref):
    rows = [taps_ref[:, block, :].astype(jnp.float32), scale_ref[block : block + 1, :], shift_ref[block : block + 1, :]]
    cols = jnp.transpose(jnp.concatenate(rows, axis=0))
    for at in range(cols.shape[1]):
        col = jnp.broadcast_to(cols[:, at : at + 1], wide_ref.shape[1:])
        if at < wide_ref.shape[0]:
            wide_ref[at] = col
        else:
            affine_ref[at - wide_ref.shape[0]] = col


def enter_kernel(
    band_in, taps_in, scale_in, shift_in, expand_in, reduce_in, bias_in,
    wide_ref, affine_ref, rows_ref, taps_ref, scale_ref, shift_ref, pack_ref, held_ref, sems,
):
    units = pack_ref.shape[2]
    moves = [(taps_in, taps_ref), (scale_in, scale_ref), (shift_in, shift_ref), (bias_in, held_ref)]
    small = len(moves)
    for block in range(BLOCKS):
        ref = pack_ref.at[block]
        moves.append((expand_in.at[block], ref.at[pl.ds(0, D)]))
        for part in range(D // units):
            columns = pl.ds(units * part, units)
            moves.append((reduce_in.at[block, :, columns], ref.at[pl.ds(D + units * part, units)]))
    moves.append((band_in, rows_ref))
    copies = [pltpu.make_async_copy(src, dst, sems.at[i]) for i, (src, dst) in enumerate(moves)]
    for copy in copies:
        copy.start()
    for copy in copies[:small]:
        copy.wait()
    spread(0, taps_ref, scale_ref, shift_ref, wide_ref, affine_ref)
    for block in range(BLOCKS):
        rest = held_ref[block : block + 1, :]
        pieces = []
        for _ in range(3):
            pieces.append(rest.astype(jnp.bfloat16))
            rest = rest - pieces[-1].astype(jnp.float32)
        pieces = [piece.astype(jnp.float32) for piece in pieces] + [jnp.zeros((5, units), jnp.float32)]
        pack_ref[block, 2 * D :, :] = jnp.concatenate(pieces, axis=0).astype(jnp.bfloat16)
    for copy in copies[small:]:
        copy.wait()


def spread_shapes(share, width):
    return tuple(jax.ShapeDtypeStruct((count, share, width), jnp.float32) for count in (TAPS * TAPS, 2))


def entered(band, taps, scale, shift, w_expand, w_reduce, b_expand):
    units = w_expand.shape[2]
    inputs = (band, taps, scale, shift, w_expand, w_reduce, b_expand)
    outs = [
        *spread_shapes(*band.shape[1:]),
        *[jax.ShapeDtypeStruct(array.shape, array.dtype) for array in inputs[:4]],
        jax.ShapeDtypeStruct((BLOCKS, 2 * D + 8, units), jnp.bfloat16),
    ]
    return pl.pallas_call(
        enter_kernel,
        out_shape=outs,
        in_specs=[pl.BlockSpec(memory_space=pltpu.HBM)] * len(inputs),
        out_specs=[VMEM] * len(outs),
        scratch_shapes=[
            pltpu.VMEM(b_expand.shape, jnp.float32),
            pltpu.SemaphoreType.DMA((5 + BLOCKS * (1 + D // units),)),
        ],
        compiler_params=pltpu.CompilerParams(vmem_limit_bytes=16 << 20),
    )(*[pltpu.with_memory_space_constraint(array, pltpu.HBM) for array in inputs])


def even_band():
    return lax.rem(lax.axis_index("space"), 2) == 0


def conv_kernel(out_first, near_ref, rows_ref, far_ref, wide_ref, out_ref):
    if out_first:
        near_ref, far_ref = far_ref, near_ref
    even = even_band()
    height, share, width = rows_ref.shape
    copies = out_ref.shape[0]
    size = 16
    column = lax.broadcasted_iota(jnp.int32, (size, width), 1)
    inside = {
        shift: ((column + shift >= 0) & (column + shift < width)).astype(jnp.float32)
        for shift in range(-HALF, HALF + 1)
    }
    for group in range(share // size):
        chans = slice(size * group, size * (group + 1))
        start = near_ref.shape[0] - HALF
        near = [near_ref[r, chans, :].astype(jnp.float32) for r in range(near_ref.shape[0])]
        far = [far_ref[r, chans, :].astype(jnp.float32) for r in range(far_ref.shape[0])]
        rows = [jnp.where(even, far[start + r], near[start + r]) for r in range(HALF)]
        rows += [rows_ref[r, chans, :] for r in range(height)]
        rows += [jnp.where(even, near[r], far[r]) for r in range(HALF)]
        rows = [row.astype(jnp.float32) for row in rows]
        totals = [None] * height
        for j in range(TAPS):
            taps = [wide_ref[i * TAPS + j, chans, :] for i in range(TAPS)]
            shift = j - HALF
            for r in range(height):
                acc = rows[r] * taps[0]
                for i in range(1, TAPS):
                    acc = acc + rows[r + i] * taps[i]
                if shift:
                    acc = pltpu.roll(acc, (-shift) % width, 1) * inside[shift]
                totals[r] = acc if totals[r] is None else totals[r] + acc
        for r in range(height):
            half, at = divmod(r, height // CORES)
            value = totals[r].astype(jnp.bfloat16)
            for copy in range(copies):
                out_ref[copy, half, chans, width * at : width * (at + 1)] = value


def hidden_of(normed, weights, unit_bias):
    preact = jnp.dot(normed, weights, preferred_element_type=jnp.float32) + unit_bias
    return (0.5 * preact * (1.0 + lax.erf(preact * (0.5**0.5)))).astype(jnp.bfloat16)


def bias_of(rows):
    pieces = rows.astype(jnp.float32)
    return pieces[0:1] + pieces[1:2] + pieces[2:3]


def normalized(block, x_ref, gain_ref, bias_ref):
    x = x_ref[...].reshape(D, x_ref.shape[-1])
    x = jnp.transpose(x).astype(jnp.float32)
    mean = jnp.mean(x, axis=-1, keepdims=True)
    centered = x - mean
    var = jnp.mean(centered * centered, axis=-1, keepdims=True)
    gain = gain_ref[block : block + 1, :]
    bias = bias_ref[block : block + 1, :]
    return (centered * lax.rsqrt(var + 1e-06) * gain + bias).astype(jnp.bfloat16)


def scatter(part, total, out_ref):
    cores, share = out_ref.shape[1:3]
    total = jnp.transpose(total.astype(jnp.bfloat16))
    count = total.shape[0] // share
    for at in range(count):
        chip, core = divmod(part * count + at, cores)
        out_ref[chip, core] = total[share * at : share * (at + 1), :]


def rows_of(part, units):
    return slice(D + units * part, D + units * (part + 1))


def mlp_kernel(block, x_ref, gain_ref, bias_ref, expand_ref, reduce_ref, unit_bias_ref, pack_ref, out_ref):
    normed = normalized(block, x_ref, gain_ref, bias_ref)
    own = hidden_of(normed, expand_ref[block], unit_bias_ref[block : block + 1, :])
    other = hidden_of(normed, pack_ref[block, :D, :], bias_of(pack_ref[block, 2 * D :, :]))
    units = own.shape[1]
    for part in range(D // units):
        own_weights = reduce_ref[block, :, units * part : units * (part + 1)]
        total = jnp.dot(own, own_weights, preferred_element_type=jnp.float32) + jnp.dot(
            other, pack_ref[block, rows_of(part, units), :], preferred_element_type=jnp.float32
        )
        scatter(part, total, out_ref)


def mix_kernel(parts_ref, stream_ref, affine_ref, out_ref, *edge_refs):
    height, share, width = stream_ref.shape
    scale, shift = affine_ref[0], affine_ref[1]
    rows = []
    for r in range(height):
        half, at = divmod(r, height // CORES)
        lanes = slice(width * at, width * (at + 1))
        mixed = parts_ref[0, half, :, lanes].astype(jnp.float32)
        for copy in range(1, parts_ref.shape[0]):
            mixed = mixed + parts_ref[copy, half, :, lanes].astype(jnp.float32)
        rows.append(stream_ref[r].astype(jnp.float32) + scale * (mixed + shift))
        out_ref[r] = rows[r].astype(jnp.bfloat16)
    if edge_refs:
        even = even_band()
        near_ref, far_ref = edge_refs
        for r in range(HALF):
            top, bottom = rows[r], rows[height - HALF + r]
            near_ref[r] = jnp.where(even, bottom, top).astype(jnp.bfloat16)
            far_ref[r] = jnp.where(even, top, bottom).astype(jnp.bfloat16)


def per_device(features, depth_kernel, norm_gain, norm_bias, w_expand, b_expand, w_reduce, b_reduce, layer_scale):
    height, width, share = features.shape
    bands, members = lax.axis_size("space"), lax.axis_size("tensor")
    copies = members // CORES
    half = height // CORES * width
    units = w_expand.shape[2]
    pairs = [(i, i ^ 1) for i in range(bands)]
    others = [(i, ((i + 1) ^ 1) - 1) for i in range(1, bands - 1)]
    sibling = [(i, i ^ 1) for i in range(members)]

    stream = jnp.transpose(features, (0, 2, 1))
    taps = jnp.transpose(depth_kernel, (1, 2, 0, 3)).reshape(TAPS * TAPS, BLOCKS, share)

    near = far = stream
    for block in range(BLOCKS):
        far = lax.ppermute(far, "space", others)
        near = lax.ppermute(near, "space", pairs)
        if block == 0:
            wide, affine, stream, taps, layer_scale, b_reduce, pack = entered(
                stream, taps, layer_scale, b_reduce, w_expand, w_reduce, b_expand
            )
            pack = lax.ppermute(pack, "tensor", sibling)
        else:
            stream, next_scale = lax.optimization_barrier((stream, layer_scale))
            wide, affine = call(
                lambda *refs: spread(1, *refs), spread_shapes(share, width), taps, next_scale, b_reduce
            )
        edges = (near, far) if block == 0 else (far, near)
        filtered = call(
            lambda *refs: conv_kernel(block > 0, *refs),
            jax.ShapeDtypeStruct((copies, CORES, share, half), jnp.bfloat16),
            edges[0], stream, edges[1], wide,
            cost=pl.CostEstimate(flops=10**11, transcendentals=0, bytes_accessed=10**6) if block == 0 else None,
        )
        filtered = lax.all_to_all(filtered.reshape(members, share, half), "tensor", 0, 0, tiled=True)
        out = jax.ShapeDtypeStruct((copies, CORES, share, half), jnp.bfloat16)
        partial = call(
            lambda *refs: mlp_kernel(block, *refs),
            out,
            filtered, norm_gain, norm_bias, w_expand, w_reduce, b_expand, pack,
        )
        partial = lax.all_to_all(partial.reshape(members, share, half), "tensor", 0, 0, tiled=True)
        partial = partial.reshape(copies, CORES, share, half)
        whole = jax.ShapeDtypeStruct((height, share, width), jnp.bfloat16)
        if block + 1 < BLOCKS:
            edge = jax.ShapeDtypeStruct((HALF, share, width), jnp.bfloat16)
            stream, near, far = call(mix_kernel, (whole, edge, edge), partial, stream, affine)
        else:
            stream = call(mix_kernel, whole, partial, stream, affine)
    return jnp.transpose(stream, (0, 2, 1))


def solution(mesh):
    return jax.shard_map(
        per_device,
        mesh=mesh,
        in_specs=(
            P("space", None, "tensor"),
            P(None, None, None, "tensor"),
            P(),
            P(),
            P(None, None, "tensor"),
            P(None, "tensor"),
            P(None, "tensor", None),
            P(None, "tensor"),
            P(None, "tensor"),
        ),
        out_specs=P("space", None, "tensor"),
        check_vma=False,
    )
```

```python
import jax
import jax.numpy as jnp
from jax import lax
from jax.experimental import pallas as pl
from jax.experimental.pallas import tpu as pltpu
from jax.sharding import PartitionSpec as P

D = 1024
TAPS = 7
HALF = TAPS // 2
BLOCKS = 2
CORES = 2

VMEM = pl.BlockSpec(memory_space=pltpu.VMEM)


def call(body, outs, *args, cost=None):
    single = not isinstance(outs, (list, tuple))
    return pl.pallas_call(
        body,
        out_shape=outs,
        in_specs=[VMEM] * len(args),
        out_specs=VMEM if single else [VMEM] * len(outs),
        cost_estimate=cost,
        compiler_params=pltpu.CompilerParams(vmem_limit_bytes=16 << 20),
    )(*args)


def spread(block, taps_ref, scale_ref, shift_ref, wide_ref, affine_ref):
    rows = [taps_ref[:, block, :].astype(jnp.float32), scale_ref[block : block + 1, :], shift_ref[block : block + 1, :]]
    cols = jnp.transpose(jnp.concatenate(rows, axis=0))
    for at in range(cols.shape[1]):
        col = jnp.broadcast_to(cols[:, at : at + 1], wide_ref.shape[1:])
        if at < wide_ref.shape[0]:
            wide_ref[at] = col
        else:
            affine_ref[at - wide_ref.shape[0]] = col


def enter_kernel(
    band_in, taps_in, scale_in, shift_in, expand_in, reduce_in, bias_in,
    wide_ref, affine_ref, rows_ref, taps_ref, scale_ref, shift_ref, pack_ref, held_ref, sems,
):
    units = pack_ref.shape[2]
    moves = [(taps_in, taps_ref), (scale_in, scale_ref), (shift_in, shift_ref), (bias_in, held_ref)]
    small = len(moves)
    for block in range(BLOCKS):
        ref = pack_ref.at[block]
        moves.append((expand_in.at[block], ref.at[pl.ds(0, D)]))
        for part in range(D // units):
            columns = pl.ds(units * part, units)
            moves.append((reduce_in.at[block, :, columns], ref.at[pl.ds(D + units * part, units)]))
    moves.append((band_in, rows_ref))
    copies = [pltpu.make_async_copy(src, dst, sems.at[i]) for i, (src, dst) in enumerate(moves)]
    for copy in copies:
        copy.start()
    for copy in copies[:small]:
        copy.wait()
    spread(0, taps_ref, scale_ref, shift_ref, wide_ref, affine_ref)
    for block in range(BLOCKS):
        rest = held_ref[block : block + 1, :]
        pieces = []
        for _ in range(3):
            pieces.append(rest.astype(jnp.bfloat16))
            rest = rest - pieces[-1].astype(jnp.float32)
        pieces = [piece.astype(jnp.float32) for piece in pieces] + [jnp.zeros((5, units), jnp.float32)]
        pack_ref[block, 2 * D :, :] = jnp.concatenate(pieces, axis=0).astype(jnp.bfloat16)
    for copy in copies[small:]:
        copy.wait()


def spread_shapes(share, width):
    return tuple(jax.ShapeDtypeStruct((count, share, width), jnp.float32) for count in (TAPS * TAPS, 2))


def entered(band, taps, scale, shift, w_expand, w_reduce, b_expand):
    units = w_expand.shape[2]
    inputs = (band, taps, scale, shift, w_expand, w_reduce, b_expand)
    outs = [
        *spread_shapes(*band.shape[1:]),
        *[jax.ShapeDtypeStruct(array.shape, array.dtype) for array in inputs[:4]],
        jax.ShapeDtypeStruct((BLOCKS, 2 * D + 8, units), jnp.bfloat16),
    ]
    return pl.pallas_call(
        enter_kernel,
        out_shape=outs,
        in_specs=[pl.BlockSpec(memory_space=pltpu.HBM)] * len(inputs),
        out_specs=[VMEM] * len(outs),
        scratch_shapes=[
            pltpu.VMEM(b_expand.shape, jnp.float32),
            pltpu.SemaphoreType.DMA((5 + BLOCKS * (1 + D // units),)),
        ],
        compiler_params=pltpu.CompilerParams(vmem_limit_bytes=16 << 20),
    )(*[pltpu.with_memory_space_constraint(array, pltpu.HBM) for array in inputs])


def even_band():
    return lax.rem(lax.axis_index("space"), 2) == 0


def conv_kernel(paired, first_ref, rows_ref, second_ref, wide_ref, out_ref):
    even = even_band() if paired else None
    height, share, width = rows_ref.shape
    copies = out_ref.shape[0]
    size = 16
    column = lax.broadcasted_iota(jnp.int32, (size, width), 1)
    inside = {
        shift: ((column + shift >= 0) & (column + shift < width)).astype(jnp.float32)
        for shift in range(-HALF, HALF + 1)
    }
    for group in range(share // size):
        chans = slice(size * group, size * (group + 1))
        start = first_ref.shape[0] - HALF
        first = [first_ref[r, chans, :].astype(jnp.float32) for r in range(first_ref.shape[0])]
        second = [second_ref[r, chans, :].astype(jnp.float32) for r in range(second_ref.shape[0])]
        if paired:
            rows = [jnp.where(even, second[start + r], first[start + r]) for r in range(HALF)]
            last = [jnp.where(even, first[r], second[r]) for r in range(HALF)]
        else:
            rows, last = first[start:], second[:HALF]
        rows += [rows_ref[r, chans, :] for r in range(height)]
        rows += last
        rows = [row.astype(jnp.float32) for row in rows]
        totals = [None] * height
        for j in range(TAPS):
            taps = [wide_ref[i * TAPS + j, chans, :] for i in range(TAPS)]
            shift = j - HALF
            for r in range(height):
                acc = rows[r] * taps[0]
                for i in range(1, TAPS):
                    acc = acc + rows[r + i] * taps[i]
                if shift:
                    acc = pltpu.roll(acc, (-shift) % width, 1) * inside[shift]
                totals[r] = acc if totals[r] is None else totals[r] + acc
        for r in range(height):
            half, at = divmod(r, height // CORES)
            value = totals[r].astype(jnp.bfloat16)
            for copy in range(copies):
                out_ref[copy, half, chans, width * at : width * (at + 1)] = value


def hidden_of(normed, weights, unit_bias):
    preact = jnp.dot(normed, weights, preferred_element_type=jnp.float32) + unit_bias
    return (0.5 * preact * (1.0 + lax.erf(preact * (0.5**0.5)))).astype(jnp.bfloat16)


def bias_of(rows):
    pieces = rows.astype(jnp.float32)
    return pieces[0:1] + pieces[1:2] + pieces[2:3]


def normalized(block, x_ref, gain_ref, bias_ref):
    x = x_ref[...].reshape(D, x_ref.shape[-1])
    x = jnp.transpose(x).astype(jnp.float32)
    mean = jnp.mean(x, axis=-1, keepdims=True)
    centered = x - mean
    var = jnp.mean(centered * centered, axis=-1, keepdims=True)
    gain = gain_ref[block : block + 1, :]
    bias = bias_ref[block : block + 1, :]
    return (centered * lax.rsqrt(var + 1e-06) * gain + bias).astype(jnp.bfloat16)


def scatter(part, total, out_ref):
    cores, share = out_ref.shape[1:3]
    total = jnp.transpose(total.astype(jnp.bfloat16))
    count = total.shape[0] // share
    for at in range(count):
        chip, core = divmod(part * count + at, cores)
        out_ref[chip, core] = total[share * at : share * (at + 1), :]


def rows_of(part, units):
    return slice(D + units * part, D + units * (part + 1))


def mlp_kernel(block, x_ref, gain_ref, bias_ref, expand_ref, reduce_ref, unit_bias_ref, pack_ref, out_ref):
    normed = normalized(block, x_ref, gain_ref, bias_ref)
    own = hidden_of(normed, expand_ref[block], unit_bias_ref[block : block + 1, :])
    other = hidden_of(normed, pack_ref[block, :D, :], bias_of(pack_ref[block, 2 * D :, :]))
    units = own.shape[1]
    for part in range(D // units):
        own_weights = reduce_ref[block, :, units * part : units * (part + 1)]
        total = jnp.dot(own, own_weights, preferred_element_type=jnp.float32) + jnp.dot(
            other, pack_ref[block, rows_of(part, units), :], preferred_element_type=jnp.float32
        )
        scatter(part, total, out_ref)


def mix_kernel(parts_ref, stream_ref, affine_ref, out_ref, *edge_refs):
    height, share, width = stream_ref.shape
    scale, shift = affine_ref[0], affine_ref[1]
    rows = []
    for r in range(height):
        half, at = divmod(r, height // CORES)
        lanes = slice(width * at, width * (at + 1))
        mixed = parts_ref[0, half, :, lanes].astype(jnp.float32)
        for copy in range(1, parts_ref.shape[0]):
            mixed = mixed + parts_ref[copy, half, :, lanes].astype(jnp.float32)
        rows.append(stream_ref[r].astype(jnp.float32) + scale * (mixed + shift))
        out_ref[r] = rows[r].astype(jnp.bfloat16)
    for ref, start in zip(edge_refs, (height - HALF, 0)):
        for r in range(HALF):
            ref[r] = rows[start + r].astype(jnp.bfloat16)


def per_device(features, depth_kernel, norm_gain, norm_bias, w_expand, b_expand, w_reduce, b_reduce, layer_scale):
    height, width, share = features.shape
    bands, members = lax.axis_size("space"), lax.axis_size("tensor")
    copies = members // CORES
    half = height // CORES * width
    units = w_expand.shape[2]
    down = [(i, i + 1) for i in range(bands - 1)]
    up = [(j, i) for i, j in down]
    pairs = [(i, i ^ 1) for i in range(bands)]
    others = [(i, ((i + 1) ^ 1) - 1) for i in range(1, bands - 1)]
    sibling = [(i, i ^ 1) for i in range(members)]

    stream = jnp.transpose(features, (0, 2, 1))
    taps = jnp.transpose(depth_kernel, (1, 2, 0, 3)).reshape(TAPS * TAPS, BLOCKS, share)

    for block in range(BLOCKS):
        if block == 0:
            second = lax.ppermute(stream, "space", others)
            first = lax.ppermute(stream, "space", pairs)
        else:
            first = lax.ppermute(last_rows, "space", down)
            second = lax.ppermute(first_rows, "space", up)
        if block == 0:
            wide, affine, stream, taps, layer_scale, b_reduce, pack = entered(
                stream, taps, layer_scale, b_reduce, w_expand, w_reduce, b_expand
            )
            pack = lax.ppermute(pack, "tensor", sibling)
        else:
            stream, next_scale = lax.optimization_barrier((stream, layer_scale))
            wide, affine = call(
                lambda *refs: spread(1, *refs), spread_shapes(share, width), taps, next_scale, b_reduce
            )
        filtered = call(
            lambda *refs: conv_kernel(block == 0, *refs),
            jax.ShapeDtypeStruct((copies, CORES, share, half), jnp.bfloat16),
            first, stream, second, wide,
            cost=pl.CostEstimate(flops=10**11, transcendentals=0, bytes_accessed=10**6) if block == 0 else None,
        )
        filtered = lax.all_to_all(filtered.reshape(members, share, half), "tensor", 0, 0, tiled=True)
        out = jax.ShapeDtypeStruct((copies, CORES, share, half), jnp.bfloat16)
        partial = call(
            lambda *refs: mlp_kernel(block, *refs),
            out,
            filtered, norm_gain, norm_bias, w_expand, w_reduce, b_expand, pack,
        )
        partial = lax.all_to_all(partial.reshape(members, share, half), "tensor", 0, 0, tiled=True)
        partial = partial.reshape(copies, CORES, share, half)
        whole = jax.ShapeDtypeStruct((height, share, width), jnp.bfloat16)
        if block + 1 < BLOCKS:
            edge = jax.ShapeDtypeStruct((HALF, share, width), jnp.bfloat16)
            stream, last_rows, first_rows = call(mix_kernel, (whole, edge, edge), partial, stream, affine)
        else:
            stream = call(mix_kernel, whole, partial, stream, affine)
    return jnp.transpose(stream, (0, 2, 1))


def solution(mesh):
    return jax.shard_map(
        per_device,
        mesh=mesh,
        in_specs=(
            P("space", None, "tensor"),
            P(None, None, None, "tensor"),
            P(),
            P(),
            P(None, None, "tensor"),
            P(None, "tensor"),
            P(None, "tensor", None),
            P(None, "tensor"),
            P(None, "tensor"),
        ),
        out_specs=P("space", None, "tensor"),
        check_vma=False,
    )
```

```python
import jax
import jax.numpy as jnp
from jax import lax
from jax.experimental import pallas as pl
from jax.experimental.pallas import tpu as pltpu
from jax.sharding import PartitionSpec as P

D = 1024
TAPS = 7
HALF = TAPS // 2
BLOCKS = 2
CORES = 2

VMEM = pl.BlockSpec(memory_space=pltpu.VMEM)


def call(body, outs, *args, cost=None):
    single = not isinstance(outs, (list, tuple))
    return pl.pallas_call(
        body,
        out_shape=outs,
        in_specs=[VMEM] * len(args),
        out_specs=VMEM if single else [VMEM] * len(outs),
        cost_estimate=cost,
        compiler_params=pltpu.CompilerParams(vmem_limit_bytes=16 << 20),
    )(*args)


def spread(block, taps_ref, scale_ref, shift_ref, wide_ref, affine_ref):
    rows = [taps_ref[:, block, :].astype(jnp.float32), scale_ref[block : block + 1, :], shift_ref[block : block + 1, :]]
    cols = jnp.transpose(jnp.concatenate(rows, axis=0))
    for at in range(cols.shape[1]):
        col = jnp.broadcast_to(cols[:, at : at + 1], wide_ref.shape[1:])
        if at < wide_ref.shape[0]:
            wide_ref[at] = col
        else:
            affine_ref[at - wide_ref.shape[0]] = col


def enter_kernel(
    band_in, taps_in, scale_in, shift_in, expand_in, reduce_in, bias_in,
    wide_ref, affine_ref, rows_ref, taps_ref, scale_ref, shift_ref, pack_ref, held_ref, sems,
):
    units = pack_ref.shape[2]
    moves = [(taps_in, taps_ref), (scale_in, scale_ref), (shift_in, shift_ref), (bias_in, held_ref)]
    small = len(moves)
    for block in range(BLOCKS):
        ref = pack_ref.at[block]
        moves.append((expand_in.at[block], ref.at[pl.ds(0, D)]))
        for part in range(D // units):
            columns = pl.ds(units * part, units)
            moves.append((reduce_in.at[block, :, columns], ref.at[pl.ds(D + units * part, units)]))
    moves.append((band_in, rows_ref))
    copies = [pltpu.make_async_copy(src, dst, sems.at[i]) for i, (src, dst) in enumerate(moves)]
    for copy in copies:
        copy.start()
    for copy in copies[:small]:
        copy.wait()
    spread(0, taps_ref, scale_ref, shift_ref, wide_ref, affine_ref)
    for block in range(BLOCKS):
        rest = held_ref[block : block + 1, :]
        pieces = []
        for _ in range(3):
            pieces.append(rest.astype(jnp.bfloat16))
            rest = rest - pieces[-1].astype(jnp.float32)
        pieces = [piece.astype(jnp.float32) for piece in pieces] + [jnp.zeros((5, units), jnp.float32)]
        pack_ref[block, 2 * D :, :] = jnp.concatenate(pieces, axis=0).astype(jnp.bfloat16)
    for copy in copies[small:]:
        copy.wait()


def spread_shapes(share, width):
    return tuple(jax.ShapeDtypeStruct((count, share, width), jnp.float32) for count in (TAPS * TAPS, 2))


def entered(band, taps, scale, shift, w_expand, w_reduce, b_expand):
    units = w_expand.shape[2]
    inputs = (band, taps, scale, shift, w_expand, w_reduce, b_expand)
    outs = [
        *spread_shapes(*band.shape[1:]),
        *[jax.ShapeDtypeStruct(array.shape, array.dtype) for array in inputs[:4]],
        jax.ShapeDtypeStruct((BLOCKS, 2 * D + 8, units), jnp.bfloat16),
    ]
    return pl.pallas_call(
        enter_kernel,
        out_shape=outs,
        in_specs=[pl.BlockSpec(memory_space=pltpu.HBM)] * len(inputs),
        out_specs=[VMEM] * len(outs),
        scratch_shapes=[
            pltpu.VMEM(b_expand.shape, jnp.float32),
            pltpu.SemaphoreType.DMA((5 + BLOCKS * (1 + D // units),)),
        ],
        compiler_params=pltpu.CompilerParams(vmem_limit_bytes=16 << 20),
    )(*[pltpu.with_memory_space_constraint(array, pltpu.HBM) for array in inputs])


def even_band():
    return lax.rem(lax.axis_index("space"), 2) == 0


def conv_kernel(out_first, near_ref, rows_ref, far_ref, wide_ref, out_ref):
    if out_first:
        near_ref, far_ref = far_ref, near_ref
    even = even_band()
    height, share, width = rows_ref.shape
    copies = out_ref.shape[0]
    size = 16
    column = lax.broadcasted_iota(jnp.int32, (size, width), 1)
    inside = {
        shift: ((column + shift >= 0) & (column + shift < width)).astype(jnp.float32)
        for shift in range(-HALF, HALF + 1)
    }
    for group in range(share // size):
        chans = slice(size * group, size * (group + 1))
        start = near_ref.shape[0] - HALF
        near = [near_ref[r, chans, :].astype(jnp.float32) for r in range(near_ref.shape[0])]
        far = [far_ref[r, chans, :].astype(jnp.float32) for r in range(far_ref.shape[0])]
        rows = [jnp.where(even, far[start + r], near[start + r]) for r in range(HALF)]
        rows += [rows_ref[r, chans, :] for r in range(height)]
        rows += [jnp.where(even, near[r], far[r]) for r in range(HALF)]
        rows = [row.astype(jnp.float32) for row in rows]
        totals = [None] * height
        for j in range(TAPS):
            taps = [wide_ref[i * TAPS + j, chans, :] for i in range(TAPS)]
            shift = j - HALF
            for r in range(height):
                acc = rows[r] * taps[0]
                for i in range(1, TAPS):
                    acc = acc + rows[r + i] * taps[i]
                if shift:
                    acc = pltpu.roll(acc, (-shift) % width, 1) * inside[shift]
                totals[r] = acc if totals[r] is None else totals[r] + acc
        for r in range(height):
            half, at = divmod(r, height // CORES)
            value = totals[r].astype(jnp.bfloat16)
            for copy in range(copies):
                out_ref[copy, half, chans, width * at : width * (at + 1)] = value


def hidden_of(normed, weights, unit_bias):
    preact = jnp.dot(normed, weights, preferred_element_type=jnp.float32) + unit_bias
    return (0.5 * preact * (1.0 + lax.erf(preact * (0.5**0.5)))).astype(jnp.bfloat16)


def bias_of(rows):
    pieces = rows.astype(jnp.float32)
    return pieces[0:1] + pieces[1:2] + pieces[2:3]


def normalized(block, x_ref, gain_ref, bias_ref):
    x = x_ref[...].reshape(D, x_ref.shape[-1])
    x = jnp.transpose(x).astype(jnp.float32)
    mean = jnp.mean(x, axis=-1, keepdims=True)
    centered = x - mean
    var = jnp.mean(centered * centered, axis=-1, keepdims=True)
    gain = gain_ref[block : block + 1, :]
    bias = bias_ref[block : block + 1, :]
    return (centered * lax.rsqrt(var + 1e-06) * gain + bias).astype(jnp.bfloat16)


def scatter(part, total, out_ref):
    cores, share = out_ref.shape[1:3]
    total = jnp.transpose(total.astype(jnp.bfloat16))
    count = total.shape[0] // share
    for at in range(count):
        chip, core = divmod(part * count + at, cores)
        out_ref[chip, core] = total[share * at : share * (at + 1), :]


def rows_of(part, units):
    return slice(D + units * part, D + units * (part + 1))


def mlp_kernel(block, x_ref, gain_ref, bias_ref, expand_ref, reduce_ref, unit_bias_ref, pack_ref, out_ref):
    normed = normalized(block, x_ref, gain_ref, bias_ref)
    own = hidden_of(normed, expand_ref[block], unit_bias_ref[block : block + 1, :])
    other = hidden_of(normed, pack_ref[block, :D, :], bias_of(pack_ref[block, 2 * D :, :]))
    units = own.shape[1]
    for part in range(D // units):
        own_weights = reduce_ref[block, :, units * part : units * (part + 1)]
        total = jnp.dot(own, own_weights, preferred_element_type=jnp.float32) + jnp.dot(
            other, pack_ref[block, rows_of(part, units), :], preferred_element_type=jnp.float32
        )
        scatter(part, total, out_ref)


def mixed_row(r, parts_ref, stream_ref, affine_ref):
    height, _, width = stream_ref.shape
    half, at = divmod(r, height // CORES)
    lanes = slice(width * at, width * (at + 1))
    mixed = parts_ref[0, half, :, lanes].astype(jnp.float32)
    for copy in range(1, parts_ref.shape[0]):
        mixed = mixed + parts_ref[copy, half, :, lanes].astype(jnp.float32)
    return stream_ref[r].astype(jnp.float32) + affine_ref[0] * (mixed + affine_ref[1])


def mix_kernel(parts_ref, stream_ref, affine_ref, out_ref, near_ref, far_ref):
    height = stream_ref.shape[0]
    rows = [mixed_row(r, parts_ref, stream_ref, affine_ref) for r in range(height)]
    for r in range(height):
        out_ref[r] = rows[r].astype(jnp.bfloat16)
    even = even_band()
    for r in range(HALF):
        top, bottom = rows[r], rows[height - HALF + r]
        near_ref[r] = jnp.where(even, bottom, top).astype(jnp.bfloat16)
        far_ref[r] = jnp.where(even, top, bottom).astype(jnp.bfloat16)


def last_kernel(parts_ref, stream_ref, affine_ref, out_ref, held_ref, sems):
    copies = []
    for r in range(stream_ref.shape[0]):
        held_ref[r] = mixed_row(r, parts_ref, stream_ref, affine_ref).astype(jnp.bfloat16)
        copies.append(pltpu.make_async_copy(held_ref.at[r], out_ref.at[r], sems.at[r]))
        copies[-1].start()
    for copy in copies:
        copy.wait()


def finish(parts, stream, affine):
    return pl.pallas_call(
        last_kernel,
        out_shape=jax.ShapeDtypeStruct(stream.shape, stream.dtype),
        in_specs=[VMEM] * 3,
        out_specs=pl.BlockSpec(memory_space=pltpu.HBM),
        scratch_shapes=[pltpu.VMEM(stream.shape, stream.dtype), pltpu.SemaphoreType.DMA((stream.shape[0],))],
        compiler_params=pltpu.CompilerParams(vmem_limit_bytes=16 << 20),
    )(parts, stream, affine)


def per_device(features, depth_kernel, norm_gain, norm_bias, w_expand, b_expand, w_reduce, b_reduce, layer_scale):
    height, width, share = features.shape
    bands, members = lax.axis_size("space"), lax.axis_size("tensor")
    copies = members // CORES
    half = height // CORES * width
    units = w_expand.shape[2]
    pairs = [(i, i ^ 1) for i in range(bands)]
    others = [(i, ((i + 1) ^ 1) - 1) for i in range(1, bands - 1)]
    sibling = [(i, i ^ 1) for i in range(members)]

    stream = jnp.transpose(features, (0, 2, 1))
    taps = jnp.transpose(depth_kernel, (1, 2, 0, 3)).reshape(TAPS * TAPS, BLOCKS, share)

    near = far = stream
    for block in range(BLOCKS):
        far = lax.ppermute(far, "space", others)
        near = lax.ppermute(near, "space", pairs)
        if block == 0:
            wide, affine, stream, taps, layer_scale, b_reduce, pack = entered(
                stream, taps, layer_scale, b_reduce, w_expand, w_reduce, b_expand
            )
            pack = lax.ppermute(pack, "tensor", sibling)
        else:
            stream, next_scale = lax.optimization_barrier((stream, layer_scale))
            wide, affine = call(
                lambda *refs: spread(1, *refs), spread_shapes(share, width), taps, next_scale, b_reduce
            )
        edges = (near, far) if block == 0 else (far, near)
        filtered = call(
            lambda *refs: conv_kernel(block > 0, *refs),
            jax.ShapeDtypeStruct((copies, CORES, share, half), jnp.bfloat16),
            edges[0], stream, edges[1], wide,
            cost=pl.CostEstimate(flops=10**11, transcendentals=0, bytes_accessed=10**6) if block == 0 else None,
        )
        filtered = lax.all_to_all(filtered.reshape(members, share, half), "tensor", 0, 0, tiled=True)
        out = jax.ShapeDtypeStruct((copies, CORES, share, half), jnp.bfloat16)
        partial = call(
            lambda *refs: mlp_kernel(block, *refs),
            out,
            filtered, norm_gain, norm_bias, w_expand, w_reduce, b_expand, pack,
        )
        partial = lax.all_to_all(partial.reshape(members, share, half), "tensor", 0, 0, tiled=True)
        partial = partial.reshape(copies, CORES, share, half)
        whole = jax.ShapeDtypeStruct((height, share, width), jnp.bfloat16)
        if block + 1 < BLOCKS:
            edge = jax.ShapeDtypeStruct((HALF, share, width), jnp.bfloat16)
            stream, near, far = call(mix_kernel, (whole, edge, edge), partial, stream, affine)
        else:
            stream = finish(partial, stream, affine)
    return jnp.transpose(stream, (0, 2, 1))


def solution(mesh):
    return jax.shard_map(
        per_device,
        mesh=mesh,
        in_specs=(
            P("space", None, "tensor"),
            P(None, None, None, "tensor"),
            P(),
            P(),
            P(None, None, "tensor"),
            P(None, "tensor"),
            P(None, "tensor", None),
            P(None, "tensor"),
            P(None, "tensor"),
        ),
        out_specs=P("space", None, "tensor"),
        check_vma=False,
    )
```

```python
import jax
import jax.numpy as jnp
from jax import lax
from jax.experimental import pallas as pl
from jax.experimental.pallas import tpu as pltpu
from jax.sharding import PartitionSpec as P

D = 1024
TAPS = 7
HALF = TAPS // 2
BLOCKS = 2
CORES = 2

VMEM = pl.BlockSpec(memory_space=pltpu.VMEM)


def call(body, outs, *args, cost=None):
    single = not isinstance(outs, (list, tuple))
    return pl.pallas_call(
        body,
        out_shape=outs,
        in_specs=[VMEM] * len(args),
        out_specs=VMEM if single else [VMEM] * len(outs),
        cost_estimate=cost,
        compiler_params=pltpu.CompilerParams(vmem_limit_bytes=16 << 20),
    )(*args)


def spread(block, taps_ref, scale_ref, shift_ref, wide_ref, affine_ref):
    rows = [taps_ref[:, block, :].astype(jnp.float32), scale_ref[block : block + 1, :], shift_ref[block : block + 1, :]]
    cols = jnp.transpose(jnp.concatenate(rows, axis=0))
    for at in range(cols.shape[1]):
        col = jnp.broadcast_to(cols[:, at : at + 1], wide_ref.shape[1:])
        if at < wide_ref.shape[0]:
            wide_ref[at] = col
        else:
            affine_ref[at - wide_ref.shape[0]] = col


def enter_kernel(
    band_in, taps_in, scale_in, shift_in, expand_in, reduce_in, bias_in,
    wide_ref, affine_ref, rows_ref, taps_ref, scale_ref, shift_ref, pack_ref, held_ref, sems,
):
    units = pack_ref.shape[2]
    moves = [(taps_in, taps_ref), (scale_in, scale_ref), (shift_in, shift_ref), (bias_in, held_ref)]
    small = len(moves)
    for block in range(BLOCKS):
        ref = pack_ref.at[block]
        moves.append((expand_in.at[block], ref.at[pl.ds(0, D)]))
        for part in range(D // units):
            columns = pl.ds(units * part, units)
            moves.append((reduce_in.at[block, :, columns], ref.at[pl.ds(D + units * part, units)]))
    moves.append((band_in, rows_ref))
    copies = [pltpu.make_async_copy(src, dst, sems.at[i]) for i, (src, dst) in enumerate(moves)]
    for copy in copies:
        copy.start()
    for copy in copies[:small]:
        copy.wait()
    spread(0, taps_ref, scale_ref, shift_ref, wide_ref, affine_ref)
    for block in range(BLOCKS):
        rest = held_ref[block : block + 1, :]
        pieces = []
        for _ in range(3):
            pieces.append(rest.astype(jnp.bfloat16))
            rest = rest - pieces[-1].astype(jnp.float32)
        pieces = [piece.astype(jnp.float32) for piece in pieces] + [jnp.zeros((5, units), jnp.float32)]
        pack_ref[block, 2 * D :, :] = jnp.concatenate(pieces, axis=0).astype(jnp.bfloat16)
    for copy in copies[small:]:
        copy.wait()


def spread_shapes(share, width):
    return tuple(jax.ShapeDtypeStruct((count, share, width), jnp.float32) for count in (TAPS * TAPS, 2))


def entered(band, taps, scale, shift, w_expand, w_reduce, b_expand):
    units = w_expand.shape[2]
    inputs = (band, taps, scale, shift, w_expand, w_reduce, b_expand)
    outs = [
        *spread_shapes(*band.shape[1:]),
        *[jax.ShapeDtypeStruct(array.shape, array.dtype) for array in inputs[:4]],
        jax.ShapeDtypeStruct((BLOCKS, 2 * D + 8, units), jnp.bfloat16),
    ]
    return pl.pallas_call(
        enter_kernel,
        out_shape=outs,
        in_specs=[pl.BlockSpec(memory_space=pltpu.HBM)] * len(inputs),
        out_specs=[VMEM] * len(outs),
        scratch_shapes=[
            pltpu.VMEM(b_expand.shape, jnp.float32),
            pltpu.SemaphoreType.DMA((5 + BLOCKS * (1 + D // units),)),
        ],
        compiler_params=pltpu.CompilerParams(vmem_limit_bytes=16 << 20),
    )(*[pltpu.with_memory_space_constraint(array, pltpu.HBM) for array in inputs])


def even_band():
    return lax.rem(lax.axis_index("space"), 2) == 0


def conv_kernel(out_first, near_ref, rows_ref, far_ref, wide_ref, out_ref):
    if out_first:
        near_ref, far_ref = far_ref, near_ref
    even = even_band()
    height, share, width = rows_ref.shape
    copies = out_ref.shape[0]
    size = 16
    column = lax.broadcasted_iota(jnp.int32, (size, width), 1)
    inside = {
        shift: ((column + shift >= 0) & (column + shift < width)).astype(jnp.float32)
        for shift in range(-HALF, HALF + 1)
    }
    for group in range(share // size):
        chans = slice(size * group, size * (group + 1))
        start = near_ref.shape[0] - HALF
        near = [near_ref[r, chans, :].astype(jnp.float32) for r in range(near_ref.shape[0])]
        far = [far_ref[r, chans, :].astype(jnp.float32) for r in range(far_ref.shape[0])]
        rows = [jnp.where(even, far[start + r], near[start + r]) for r in range(HALF)]
        rows += [rows_ref[r, chans, :] for r in range(height)]
        rows += [jnp.where(even, near[r], far[r]) for r in range(HALF)]
        rows = [row.astype(jnp.float32) for row in rows]
        totals = [None] * height
        for j in range(TAPS):
            taps = [wide_ref[i * TAPS + j, chans, :] for i in range(TAPS)]
            shift = j - HALF
            for r in range(height):
                acc = rows[r] * taps[0]
                for i in range(1, TAPS):
                    acc = acc + rows[r + i] * taps[i]
                if shift:
                    acc = pltpu.roll(acc, (-shift) % width, 1) * inside[shift]
                totals[r] = acc if totals[r] is None else totals[r] + acc
        for r in range(height):
            half, at = divmod(r, height // CORES)
            value = totals[r].astype(jnp.bfloat16)
            for copy in range(copies):
                out_ref[copy, half, chans, width * at : width * (at + 1)] = value


def hidden_of(normed, weights, unit_bias):
    preact = jnp.dot(normed, weights, preferred_element_type=jnp.float32) + unit_bias
    return (0.5 * preact * (1.0 + lax.erf(preact * (0.5**0.5)))).astype(jnp.bfloat16)


def bias_of(rows):
    pieces = rows.astype(jnp.float32)
    return pieces[0:1] + pieces[1:2] + pieces[2:3]


def normalized(block, x_ref, gain_ref, bias_ref):
    x = x_ref[...].reshape(D, x_ref.shape[-1])
    x = jnp.transpose(x).astype(jnp.float32)
    mean = jnp.mean(x, axis=-1, keepdims=True)
    centered = x - mean
    var = jnp.mean(centered * centered, axis=-1, keepdims=True)
    gain = gain_ref[block : block + 1, :]
    bias = bias_ref[block : block + 1, :]
    return (centered * lax.rsqrt(var + 1e-06) * gain + bias).astype(jnp.bfloat16)


def scatter(part, total, out_ref):
    cores, share = out_ref.shape[1:3]
    total = jnp.transpose(total.astype(jnp.bfloat16))
    count = total.shape[0] // share
    for at in range(count):
        chip, core = divmod(part * count + at, cores)
        out_ref[chip, core] = total[share * at : share * (at + 1), :]


def rows_of(part, units):
    return slice(D + units * part, D + units * (part + 1))


def mlp_kernel(block, x_ref, gain_ref, bias_ref, expand_ref, reduce_ref, unit_bias_ref, pack_ref, out_ref):
    normed = normalized(block, x_ref, gain_ref, bias_ref)
    own = hidden_of(normed, expand_ref[block], unit_bias_ref[block : block + 1, :])
    other = hidden_of(normed, pack_ref[block, :D, :], bias_of(pack_ref[block, 2 * D :, :]))
    units = own.shape[1]
    for part in range(D // units):
        own_weights = reduce_ref[block, :, units * part : units * (part + 1)]
        total = jnp.dot(own, own_weights, preferred_element_type=jnp.float32) + jnp.dot(
            other, pack_ref[block, rows_of(part, units), :], preferred_element_type=jnp.float32
        )
        scatter(part, total, out_ref)


def mix_kernel(parts_ref, stream_ref, affine_ref, out_ref, *edge_refs):
    height, share, width = stream_ref.shape
    scale, shift = affine_ref[0], affine_ref[1]
    rows = []
    for r in range(height):
        half, at = divmod(r, height // CORES)
        lanes = slice(width * at, width * (at + 1))
        mixed = parts_ref[0, half, :, lanes].astype(jnp.float32)
        for copy in range(1, parts_ref.shape[0]):
            mixed = mixed + parts_ref[copy, half, :, lanes].astype(jnp.float32)
        rows.append(stream_ref[r].astype(jnp.float32) + scale * (mixed + shift))
        out_ref[r] = rows[r].astype(jnp.bfloat16)
    if edge_refs:
        even = even_band()
        near_ref, far_ref = edge_refs
        for r in range(HALF):
            top, bottom = rows[r], rows[height - HALF + r]
            near_ref[r] = jnp.where(even, bottom, top).astype(jnp.bfloat16)
            far_ref[r] = jnp.where(even, top, bottom).astype(jnp.bfloat16)


def per_device(features, depth_kernel, norm_gain, norm_bias, w_expand, b_expand, w_reduce, b_reduce, layer_scale):
    height, width, share = features.shape
    bands, members = lax.axis_size("space"), lax.axis_size("tensor")
    copies = members // CORES
    half = height // CORES * width
    units = w_expand.shape[2]
    pairs = [(i, i ^ 1) for i in range(bands)]
    others = [(i, ((i + 1) ^ 1) - 1) for i in range(1, bands - 1)]
    sibling = [(i, i ^ 1) for i in range(members)]

    stream = jnp.transpose(features, (0, 2, 1))
    taps = jnp.transpose(depth_kernel, (1, 2, 0, 3)).reshape(TAPS * TAPS, BLOCKS, share)

    near = far = stream
    for block in range(BLOCKS):
        far = lax.ppermute(far, "space", others)
        if block == 0:
            wide, affine, stream, taps, layer_scale, b_reduce, pack = entered(
                stream, taps, layer_scale, b_reduce, w_expand, w_reduce, b_expand
            )
            near = lax.ppermute(stream, "space", pairs)
            pack = lax.ppermute(pack, "tensor", sibling)
        else:
            near = lax.ppermute(near, "space", pairs)
            stream, next_scale = lax.optimization_barrier((stream, layer_scale))
            wide, affine = call(
                lambda *refs: spread(1, *refs), spread_shapes(share, width), taps, next_scale, b_reduce
            )
        edges = (near, far) if block == 0 else (far, near)
        filtered = call(
            lambda *refs: conv_kernel(block > 0, *refs),
            jax.ShapeDtypeStruct((copies, CORES, share, half), jnp.bfloat16),
            edges[0], stream, edges[1], wide,
            cost=pl.CostEstimate(flops=10**11, transcendentals=0, bytes_accessed=10**6) if block == 0 else None,
        )
        filtered = lax.all_to_all(filtered.reshape(members, share, half), "tensor", 0, 0, tiled=True)
        out = jax.ShapeDtypeStruct((copies, CORES, share, half), jnp.bfloat16)
        partial = call(
            lambda *refs: mlp_kernel(block, *refs),
            out,
            filtered, norm_gain, norm_bias, w_expand, w_reduce, b_expand, pack,
        )
        partial = lax.all_to_all(partial.reshape(members, share, half), "tensor", 0, 0, tiled=True)
        partial = partial.reshape(copies, CORES, share, half)
        whole = jax.ShapeDtypeStruct((height, share, width), jnp.bfloat16)
        if block + 1 < BLOCKS:
            edge = jax.ShapeDtypeStruct((HALF, share, width), jnp.bfloat16)
            stream, near, far = call(mix_kernel, (whole, edge, edge), partial, stream, affine)
        else:
            stream = call(mix_kernel, whole, partial, stream, affine)
    return jnp.transpose(stream, (0, 2, 1))


def solution(mesh):
    return jax.shard_map(
        per_device,
        mesh=mesh,
        in_specs=(
            P("space", None, "tensor"),
            P(None, None, None, "tensor"),
            P(),
            P(),
            P(None, None, "tensor"),
            P(None, "tensor"),
            P(None, "tensor", None),
            P(None, "tensor"),
            P(None, "tensor"),
        ),
        out_specs=P("space", None, "tensor"),
        check_vma=False,
    )
```

```python
import jax
import jax.numpy as jnp
from jax import lax
from jax.experimental import pallas as pl
from jax.experimental.pallas import tpu as pltpu
from jax.sharding import PartitionSpec as P

D = 1024
TAPS = 7
HALF = TAPS // 2
BLOCKS = 2
CORES = 2

VMEM = pl.BlockSpec(memory_space=pltpu.VMEM)


def call(body, outs, *args, cost=None):
    single = not isinstance(outs, (list, tuple))
    return pl.pallas_call(
        body,
        out_shape=outs,
        in_specs=[VMEM] * len(args),
        out_specs=VMEM if single else [VMEM] * len(outs),
        cost_estimate=cost,
        compiler_params=pltpu.CompilerParams(vmem_limit_bytes=16 << 20),
    )(*args)


def spread(block, taps_ref, scale_ref, shift_ref, wide_ref, affine_ref):
    rows = [taps_ref[:, block, :].astype(jnp.float32), scale_ref[block : block + 1, :], shift_ref[block : block + 1, :]]
    cols = jnp.transpose(jnp.concatenate(rows, axis=0))
    for at in range(cols.shape[1]):
        col = jnp.broadcast_to(cols[:, at : at + 1], wide_ref.shape[1:])
        if at < wide_ref.shape[0]:
            wide_ref[at] = col
        else:
            affine_ref[at - wide_ref.shape[0]] = col


def enter_kernel(
    band_in, taps_in, scale_in, shift_in, expand_in, reduce_in, bias_in,
    wide_ref, affine_ref, rows_ref, taps_ref, scale_ref, shift_ref, pack_ref, held_ref, sems,
):
    units = pack_ref.shape[2]
    moves = [(taps_in, taps_ref), (scale_in, scale_ref), (shift_in, shift_ref), (bias_in, held_ref)]
    small = len(moves)
    for block in range(BLOCKS):
        ref = pack_ref.at[block]
        moves.append((expand_in.at[block], ref.at[pl.ds(0, D)]))
        for part in range(D // units):
            columns = pl.ds(units * part, units)
            moves.append((reduce_in.at[block, :, columns], ref.at[pl.ds(D + units * part, units)]))
    moves.append((band_in, rows_ref))
    copies = [pltpu.make_async_copy(src, dst, sems.at[i]) for i, (src, dst) in enumerate(moves)]
    for copy in copies:
        copy.start()
    for copy in copies[:small]:
        copy.wait()
    spread(0, taps_ref, scale_ref, shift_ref, wide_ref, affine_ref)
    for block in range(BLOCKS):
        rest = held_ref[block : block + 1, :]
        pieces = []
        for _ in range(3):
            pieces.append(rest.astype(jnp.bfloat16))
            rest = rest - pieces[-1].astype(jnp.float32)
        pieces = [piece.astype(jnp.float32) for piece in pieces] + [jnp.zeros((5, units), jnp.float32)]
        pack_ref[block, 2 * D :, :] = jnp.concatenate(pieces, axis=0).astype(jnp.bfloat16)
    for copy in copies[small:]:
        copy.wait()


def spread_shapes(share, width):
    return tuple(jax.ShapeDtypeStruct((count, share, width), jnp.float32) for count in (TAPS * TAPS, 2))


def entered(band, taps, scale, shift, w_expand, w_reduce, b_expand):
    units = w_expand.shape[2]
    inputs = (band, taps, scale, shift, w_expand, w_reduce, b_expand)
    outs = [
        *spread_shapes(*band.shape[1:]),
        *[jax.ShapeDtypeStruct(array.shape, array.dtype) for array in inputs[:4]],
        jax.ShapeDtypeStruct((BLOCKS, 2 * D + 8, units), jnp.bfloat16),
    ]
    return pl.pallas_call(
        enter_kernel,
        out_shape=outs,
        in_specs=[pl.BlockSpec(memory_space=pltpu.HBM)] * len(inputs),
        out_specs=[VMEM] * len(outs),
        scratch_shapes=[
            pltpu.VMEM(b_expand.shape, jnp.float32),
            pltpu.SemaphoreType.DMA((5 + BLOCKS * (1 + D // units),)),
        ],
        compiler_params=pltpu.CompilerParams(vmem_limit_bytes=16 << 20),
    )(*[pltpu.with_memory_space_constraint(array, pltpu.HBM) for array in inputs])


def even_band():
    return lax.rem(lax.axis_index("space"), 2) == 0


def conv_kernel(out_first, near_ref, rows_ref, far_ref, wide_ref, out_ref):
    if out_first:
        near_ref, far_ref = far_ref, near_ref
    even = even_band()
    height, share, width = rows_ref.shape
    copies = out_ref.shape[0]
    size = 16
    column = lax.broadcasted_iota(jnp.int32, (size, width), 1)
    inside = {
        shift: ((column + shift >= 0) & (column + shift < width)).astype(jnp.float32)
        for shift in range(-HALF, HALF + 1)
    }
    for group in range(share // size):
        chans = slice(size * group, size * (group + 1))
        start = near_ref.shape[0] - HALF
        near = [near_ref[r, chans, :].astype(jnp.float32) for r in range(near_ref.shape[0])]
        far = [far_ref[r, chans, :].astype(jnp.float32) for r in range(far_ref.shape[0])]
        rows = [jnp.where(even, far[start + r], near[start + r]) for r in range(HALF)]
        rows += [rows_ref[r, chans, :] for r in range(height)]
        rows += [jnp.where(even, near[r], far[r]) for r in range(HALF)]
        rows = [row.astype(jnp.float32) for row in rows]
        totals = [None] * height
        for j in range(TAPS):
            taps = [wide_ref[i * TAPS + j, chans, :] for i in range(TAPS)]
            shift = j - HALF
            for r in range(height):
                acc = rows[r] * taps[0]
                for i in range(1, TAPS):
                    acc = acc + rows[r + i] * taps[i]
                if shift:
                    acc = pltpu.roll(acc, (-shift) % width, 1) * inside[shift]
                totals[r] = acc if totals[r] is None else totals[r] + acc
        for r in range(height):
            half, at = divmod(r, height // CORES)
            value = totals[r].astype(jnp.bfloat16)
            for copy in range(copies):
                out_ref[copy, half, chans, width * at : width * (at + 1)] = value


def hidden_of(normed, weights, unit_bias):
    preact = jnp.dot(normed, weights, preferred_element_type=jnp.float32) + unit_bias
    return (0.5 * preact * (1.0 + lax.erf(preact * (0.5**0.5)))).astype(jnp.bfloat16)


def bias_of(rows):
    pieces = rows.astype(jnp.float32)
    return pieces[0:1] + pieces[1:2] + pieces[2:3]


def normalized(block, x_ref, gain_ref, bias_ref):
    whole = jnp.transpose(x_ref[...].reshape(D, x_ref.shape[-1]))
    gain = gain_ref[block : block + 1, :]
    bias = bias_ref[block : block + 1, :]
    size = 16
    groups = []
    for at in range(0, whole.shape[0], size):
        x = whole[at : at + size, :].astype(jnp.float32)
        mean = jnp.mean(x, axis=-1, keepdims=True)
        centered = x - mean
        var = jnp.mean(centered * centered, axis=-1, keepdims=True)
        groups.append((centered * lax.rsqrt(var + 1e-06) * gain + bias).astype(jnp.bfloat16))
    return jnp.concatenate(groups, axis=0)


def scatter(part, total, out_ref):
    cores, share = out_ref.shape[1:3]
    total = jnp.transpose(total.astype(jnp.bfloat16))
    count = total.shape[0] // share
    for at in range(count):
        chip, core = divmod(part * count + at, cores)
        out_ref[chip, core] = total[share * at : share * (at + 1), :]


def rows_of(part, units):
    return slice(D + units * part, D + units * (part + 1))


def mlp_kernel(block, x_ref, gain_ref, bias_ref, expand_ref, reduce_ref, unit_bias_ref, pack_ref, out_ref):
    normed = normalized(block, x_ref, gain_ref, bias_ref)
    own = hidden_of(normed, expand_ref[block], unit_bias_ref[block : block + 1, :])
    other = hidden_of(normed, pack_ref[block, :D, :], bias_of(pack_ref[block, 2 * D :, :]))
    units = own.shape[1]
    for part in range(D // units):
        own_weights = reduce_ref[block, :, units * part : units * (part + 1)]
        total = jnp.dot(own, own_weights, preferred_element_type=jnp.float32) + jnp.dot(
            other, pack_ref[block, rows_of(part, units), :], preferred_element_type=jnp.float32
        )
        scatter(part, total, out_ref)


def mix_kernel(parts_ref, stream_ref, affine_ref, out_ref, *edge_refs):
    height, share, width = stream_ref.shape
    scale, shift = affine_ref[0], affine_ref[1]
    rows = []
    for r in range(height):
        half, at = divmod(r, height // CORES)
        lanes = slice(width * at, width * (at + 1))
        mixed = parts_ref[0, half, :, lanes].astype(jnp.float32)
        for copy in range(1, parts_ref.shape[0]):
            mixed = mixed + parts_ref[copy, half, :, lanes].astype(jnp.float32)
        rows.append(stream_ref[r].astype(jnp.float32) + scale * (mixed + shift))
        out_ref[r] = rows[r].astype(jnp.bfloat16)
    if edge_refs:
        even = even_band()
        near_ref, far_ref = edge_refs
        for r in range(HALF):
            top, bottom = rows[r], rows[height - HALF + r]
            near_ref[r] = jnp.where(even, bottom, top).astype(jnp.bfloat16)
            far_ref[r] = jnp.where(even, top, bottom).astype(jnp.bfloat16)


def per_device(features, depth_kernel, norm_gain, norm_bias, w_expand, b_expand, w_reduce, b_reduce, layer_scale):
    height, width, share = features.shape
    bands, members = lax.axis_size("space"), lax.axis_size("tensor")
    copies = members // CORES
    half = height // CORES * width
    units = w_expand.shape[2]
    pairs = [(i, i ^ 1) for i in range(bands)]
    others = [(i, ((i + 1) ^ 1) - 1) for i in range(1, bands - 1)]
    sibling = [(i, i ^ 1) for i in range(members)]

    stream = jnp.transpose(features, (0, 2, 1))
    taps = jnp.transpose(depth_kernel, (1, 2, 0, 3)).reshape(TAPS * TAPS, BLOCKS, share)

    near = far = stream
    for block in range(BLOCKS):
        far = lax.ppermute(far, "space", others)
        near = lax.ppermute(near, "space", pairs)
        if block == 0:
            wide, affine, stream, taps, layer_scale, b_reduce, pack = entered(
                stream, taps, layer_scale, b_reduce, w_expand, w_reduce, b_expand
            )
            pack = lax.ppermute(pack, "tensor", sibling)
        else:
            stream, next_scale = lax.optimization_barrier((stream, layer_scale))
            wide, affine = call(
                lambda *refs: spread(1, *refs), spread_shapes(share, width), taps, next_scale, b_reduce
            )
        edges = (near, far) if block == 0 else (far, near)
        filtered = call(
            lambda *refs: conv_kernel(block > 0, *refs),
            jax.ShapeDtypeStruct((copies, CORES, share, half), jnp.bfloat16),
            edges[0], stream, edges[1], wide,
            cost=pl.CostEstimate(flops=10**11, transcendentals=0, bytes_accessed=10**6) if block == 0 else None,
        )
        filtered = lax.all_to_all(filtered.reshape(members, share, half), "tensor", 0, 0, tiled=True)
        out = jax.ShapeDtypeStruct((copies, CORES, share, half), jnp.bfloat16)
        partial = call(
            lambda *refs: mlp_kernel(block, *refs),
            out,
            filtered, norm_gain, norm_bias, w_expand, w_reduce, b_expand, pack,
        )
        partial = lax.all_to_all(partial.reshape(members, share, half), "tensor", 0, 0, tiled=True)
        partial = partial.reshape(copies, CORES, share, half)
        whole = jax.ShapeDtypeStruct((height, share, width), jnp.bfloat16)
        if block + 1 < BLOCKS:
            edge = jax.ShapeDtypeStruct((HALF, share, width), jnp.bfloat16)
            stream, near, far = call(mix_kernel, (whole, edge, edge), partial, stream, affine)
        else:
            stream = call(mix_kernel, whole, partial, stream, affine)
    return jnp.transpose(stream, (0, 2, 1))


def solution(mesh):
    return jax.shard_map(
        per_device,
        mesh=mesh,
        in_specs=(
            P("space", None, "tensor"),
            P(None, None, None, "tensor"),
            P(),
            P(),
            P(None, None, "tensor"),
            P(None, "tensor"),
            P(None, "tensor", None),
            P(None, "tensor"),
            P(None, "tensor"),
        ),
        out_specs=P("space", None, "tensor"),
        check_vma=False,
    )
```
